128 devices in a mesh: inp: 8 (over x, z_lo), freq: 16 (over y, z_hi, core).
Axes of the slice: x: 4, y: 4, z: 4 (z_hi: 2, z_lo: 2; z = z_hi * 2 + z_lo), core: 2. Of those that a mesh axis runs over, the one named last changes fastest.
Arguments:
- volts: bfloat16 [32, 2, 4096, 1024], P('freq', None, 'inp'), parts along dimension 0, may hold values from -6 to 6
- position_input: int32 [16, 256], P('inp'), may hold values from 0 to 255, each once within a row
- tile_group: int32 [16, 4, 2], P('inp'), may hold values from 0 to 63
Outputs:
- stacked: float32 [64, 32, 2, 511], P('inp', 'freq'), parts along dimension 1
The draws below stay inside these ranges and needn't reach their ends.
There are 16 independent parts, one for each index of `freq`. The reference program is written for one: setup_inputs(seed, part) draws one part's arguments, and reference() takes and returns one part's arrays. A program takes and returns all parts, laid end to end along the dimension named above; an argument that names none is the same for every part. Nothing has to cross between parts.
Inputs may be any that keep to these rules, and one draw needn't show every extreme that they name: `position_input`: each row holds every position's input index within the block once. `tile_group`: entry [a, l, b] names the row group of the tile of block a with the b-th block of the device at level l of block a's device.
All inputs are finite; a program needn't handle non-finite values.
Results may differ from the reference program's by a relative error of at most 0.0003.
Values may be sent and summed in bfloat16 or wider, within the bound.
A program may use at most 192 MiB of HBM per device.

```python
import math
import jax
import jax.numpy as jnp
import numpy as np
from jax import lax

B = 256
BLK_DEV = 2
SAMPLES = 1024
F_DEV = 2
LEVELS = 3
NBLK = 16
INPUTS = 4096
ROWGROUPS = 64
DIFFS = 511
N_INP = 8


def with_ends(entries, stream_key, low, largest):
    shape = entries.shape
    spot = [jax.random.randint(jax.random.fold_in(stream_key, axis), (), 0, shape[axis]) for axis in range(len(shape))]
    entries = entries.at[tuple(spot)].set(low)
    longest = shape.index(max(shape))
    spot[longest] = (spot[longest] + 1) % shape[longest]
    return entries.at[tuple(spot)].set(largest)


def shard_levels(rng, dims, pieces, smallest, high):
    factor_of = 1.0
    for axis_at, blocks in pieces:
        heights = jax.random.uniform(jax.random.fold_in(jax.random.fold_in(rng, 6), axis_at), (blocks,), jnp.float32, smallest / len(pieces), high / len(pieces))
        factor_of = factor_of * jnp.repeat(jnp.exp(heights), dims[axis_at] // blocks).reshape((-1,) + (1,) * (len(dims) - 1 - axis_at))
    return factor_of


def rank_table(number_of, skew):
    loads = [(1 << 20) // math.isqrt(grade ** skew) + 1 for grade in range(1, number_of + 1)]
    deviation = 1 + sum(loads) // (1 << 30)
    return np.cumsum(np.array([max(1, weight // deviation) for weight in loads]))


def ranked_ids(key, dims, count, slope):
    grid = rank_table(count, slope)
    pick = jax.random.randint(jax.random.fold_in(key, 1), dims, 0, int(grid[count - 1]))
    standing = jnp.searchsorted(jnp.asarray(grid, jnp.int32), pick, side="right")
    return jax.random.permutation(jax.random.fold_in(key, 2), count)[standing].astype(jnp.int32)


def normal_values(key, extent, width, limit, cuts=(), kind=jnp.bfloat16):
    values = width * jax.random.normal(key, extent, jnp.float32)
    if cuts:
        values = values * shard_levels(key, extent, cuts, -0.22, 0.18)
    return jnp.clip(values, -limit, limit).astype(kind)


def setup_inputs(seed: int = 0, part: int = 0) -> dict:
    key_list = jax.random.split(jax.random.key(seed), 4)
    part_splits = jax.random.split(jax.random.fold_in(key_list[3], part), 4)
    return {
        "volts": normal_values(part_splits[0], (F_DEV, 2, INPUTS, SAMPLES), 1.0, 6.0, ((2, 8),)),
        "position_input": jax.vmap(lambda own: jax.random.permutation(own, B))(jax.random.split(key_list[1], NBLK)).reshape((NBLK, B)).astype(jnp.int32),
        "tile_group": with_ends(ranked_ids(key_list[2], (NBLK, LEVELS + 1, BLK_DEV), ROWGROUPS, 2), jax.random.fold_in(key_list[2], 3), 0, ROWGROUPS - 1).astype(jnp.int32),
    }


def diagonals(tile_block):
    tile_width = tile_block.shape[-1]
    lead = tile_block.shape[:-2]
    flipped = jnp.flip(tile_block, axis=-2)
    padded = jnp.pad(flipped, [(0, 0)] * len(lead) + [(0, 0), (0, tile_width)])
    flattened = padded.reshape(lead + (2 * tile_width * tile_width,))
    flattened = flattened[..., : tile_width * (2 * tile_width - 1)]
    sheared = flattened.reshape(lead + (tile_width, 2 * tile_width - 1))
    return jnp.sum(sheared, axis=-2)


def cross_tiles(own_panel, partner_panel):
    own_f = own_panel.astype(jnp.float32)
    partner_f = partner_panel.astype(jnp.float32)
    high = lax.Precision.HIGHEST
    real_part = jnp.einsum("fps,fqs->fpq", own_f[:, 0], partner_f[:, 0], precision=high) + jnp.einsum("fps,fqs->fpq", own_f[:, 1], partner_f[:, 1], precision=high)
    imag_part = jnp.einsum("fps,fqs->fpq", own_f[:, 1], partner_f[:, 0], precision=high) - jnp.einsum("fps,fqs->fpq", own_f[:, 0], partner_f[:, 1], precision=high)
    return real_part, imag_part


def stack_round(real_part, imag_part, own_round, blocks, tile_width, samples):
    stacked_parts = jnp.stack([real_part, imag_part], axis=1) * (1.0 / samples)
    channels = stacked_parts.shape[0]
    tile_view = stacked_parts.reshape(channels, 2, blocks, tile_width, blocks, tile_width).transpose(0, 1, 2, 4, 3, 5)
    lag_sums = diagonals(tile_view)
    if own_round:
        diffs = 2 * tile_width - 1
        center = (jnp.arange(diffs) == tile_width - 1).astype(jnp.float32)
        keep_mask = 1.0 - jnp.eye(blocks, dtype=jnp.float32)[:, :, None] * center[None, None, :]
        lag_sums = lag_sums * keep_mask
    return lag_sums


def reference(volts, position_input, tile_group):
    blocks_all, tile_width = position_input.shape
    offsets = tile_width * jnp.arange(blocks_all)[:, None]
    index_list = (position_input + offsets).reshape(-1).astype(jnp.int32)
    ordered = jnp.take(volts, index_list, axis=2)
    channels = volts.shape[0]
    samples = volts.shape[3]
    row_count = BLK_DEV * tile_width
    stacked = jnp.zeros((ROWGROUPS, channels, 2, DIFFS), jnp.float32)
    group_range = jnp.arange(ROWGROUPS).astype(jnp.int32)
    for device in range(N_INP):
        own_panel = ordered[:, :, device * row_count:(device + 1) * row_count]
        partners = [device] + [device ^ (1 << bit_index) for bit_index in range(LEVELS)]
        for level_index in range(LEVELS + 1):
            partner = partners[level_index]
            partner_panel = ordered[:, :, partner * row_count:(partner + 1) * row_count]
            real_part, imag_part = cross_tiles(own_panel, partner_panel)
            lag_sums = stack_round(real_part, imag_part, level_index == 0, BLK_DEV, tile_width, samples)
            group_ids = tile_group[device * BLK_DEV:(device + 1) * BLK_DEV, level_index, :].reshape(-1).astype(jnp.int32)
            one_hot = (group_ids[:, None] == group_range[None, :]).astype(jnp.float32)
            flat_sums = lag_sums.reshape(channels, 2, BLK_DEV * BLK_DEV, DIFFS)
            stacked = stacked + jnp.einsum("ng,fcne->gfce", one_hot, flat_sums, precision=lax.Precision.HIGHEST)
    return stacked
```

```python
import jax
import jax.numpy as jnp
from jax import lax
from jax.experimental import pallas as pl
from jax.experimental.pallas import tpu as pltpu
from jax.sharding import PartitionSpec as P

RG_DEV = 8
HIGH = lax.Precision.HIGHEST
NT = (((1,), (1,)), ((), ()))


def lag_kernel(sel_ref, x_ref, y_ref, o_ref):
    width = x_ref.shape[3]
    for a in range(2):
        xre = x_ref[0, 0, a]
        xim = x_ref[0, 1, a]
        for b in range(2):
            yre = y_ref[0, 0, b]
            yim = y_ref[0, 1, b]
            dot = lambda u, v: lax.dot_general(u, v, NT, preferred_element_type=jnp.float32)
            real_part = dot(xre, yre) + dot(xim, yim)
            imag_part = dot(xim, yre) - dot(xre, yim)
            for c, part in enumerate((real_part, imag_part)):
                padded = jnp.concatenate([part, jnp.zeros_like(part)], axis=1)
                sheared = pltpu.roll(padded, 0, 1, stride=1, stride_axis=0)
                row = (a * 2 + b) * 2 + c
                o_ref[0, pl.ds(row, 1), :] = jnp.sum(sheared, axis=0, keepdims=True)
    del width


def pair_lags(sel, x_all, y_all, y_by_sel):
    n = sel.shape[0]
    _, _, _, width, samples = x_all.shape
    x_spec = pl.BlockSpec((1, 2, 2, width, samples), lambda i, s: (s[i], 0, 0, 0, 0))
    if y_by_sel:
        y_spec = pl.BlockSpec((1, 2, 2, width, samples), lambda i, s: (s[i], 0, 0, 0, 0))
    else:
        y_spec = pl.BlockSpec((1, 2, 2, width, samples), lambda i, s: (i, 0, 0, 0, 0))
    out_spec = pl.BlockSpec((1, 8, 2 * width), lambda i, s: (i, 0, 0))
    flops = n * 16 * 2 * width * width * samples
    return pl.pallas_call(
        lag_kernel,
        out_shape=jax.ShapeDtypeStruct((n, 8, 2 * width), jnp.float32),
        grid_spec=pltpu.PrefetchScalarGridSpec(
            num_scalar_prefetch=1,
            grid=(n,),
            in_specs=[x_spec, y_spec],
            out_specs=out_spec,
        ),
        compiler_params=pltpu.CompilerParams(vmem_limit_bytes=48 * 1024 * 1024),
        cost_estimate=pl.CostEstimate(
            flops=flops, transcendentals=0, bytes_accessed=n * 2 * 4 * width * samples * 2
        ),
    )(sel, x_all, y_all)


def on_device(volts, position_input, tile_group):
    blocks, width = position_input.shape
    channels, _, _, samples = volts.shape
    diffs = 2 * width - 1
    n_inp = lax.axis_size("inp")
    levels = n_inp.bit_length() - 1
    me = lax.axis_index("inp")

    ids = jnp.arange(width, dtype=jnp.int32)
    perm = (position_input[:, :, None] == ids[None, None, :]).astype(volts.dtype)
    perm_rev = perm[:, ::-1, :]
    v5 = volts.reshape(channels, 2, blocks, width, samples)
    ordered = jnp.einsum("api,fcais->fcaps", perm, v5, preferred_element_type=jnp.float32).astype(volts.dtype)
    reversed_ = jnp.einsum("api,fcais->fcaps", perm_rev, v5, preferred_element_type=jnp.float32).astype(volts.dtype)

    groups_all = RG_DEV * n_inp
    group_ids = jnp.arange(groups_all, dtype=jnp.int32)
    tg_all = lax.all_gather(tile_group, "inp", tiled=True)

    lag0 = pair_lags(jnp.arange(channels, dtype=jnp.int32), ordered, reversed_, True)
    lag0 = lag0.reshape(channels, 2, 2, 2, 2 * width)
    center = (jnp.arange(2 * width) == width - 1)
    same = jnp.eye(2, dtype=bool)
    lag0 = jnp.where(same[None, :, :, None, None] & center[None, None, None, None, :], 0.0, lag0)
    w0 = (tile_group[:, 0, :, None] == group_ids).astype(jnp.float32)
    dense_rev = jnp.einsum("abg,fabcj->gfcj", w0, lag0, precision=HIGH)
    dense_fwd = None
    chan_ids = jnp.arange(channels, dtype=jnp.int32)
    sign = jnp.array([1.0, -1.0], jnp.float32)
    for bit in range(levels):
        partner = me ^ (1 << bit)
        mine = (me >> bit) & 1
        send = lax.dynamic_index_in_dim(reversed_, 1 - mine, axis=0, keepdims=True)
        got = lax.ppermute(send, "inp", [(i, i ^ (1 << bit)) for i in range(n_inp)])
        lag = pair_lags(mine[None].astype(jnp.int32), ordered, got, False)
        lag = lag.reshape(2, 2, 2, 2 * width)
        fmask = (chan_ids == mine).astype(jnp.float32)
        w_direct = (tile_group[:, bit + 1, :, None] == group_ids).astype(jnp.float32)
        tg_partner = lax.dynamic_slice_in_dim(tg_all, partner * blocks, blocks, axis=0)
        w_trans = (tg_partner[:, bit + 1, :, None] == group_ids).astype(jnp.float32)
        dense_rev = dense_rev + jnp.einsum("abg,f,abcj->gfcj", w_direct, fmask, lag, precision=HIGH)
        term = jnp.einsum("bag,f,c,abcj->gfcj", w_trans, fmask, sign, lag, precision=HIGH)
        dense_fwd = term if dense_fwd is None else dense_fwd + term
    dense = jnp.flip(dense_rev[..., :diffs], axis=-1) + dense_fwd[..., :diffs]
    dense = dense * (1.0 / samples)
    return lax.psum_scatter(dense, "inp", scatter_dimension=0, tiled=True)


def solution(mesh):
    return jax.shard_map(
        on_device,
        mesh=mesh,
        in_specs=(P("freq", None, "inp", None), P("inp", None), P("inp", None, None)),
        out_specs=P("inp", "freq", None, None),
        check_vma=False,
    )
```

```python
import jax
import jax.numpy as jnp
from jax import lax
from jax.experimental import pallas as pl
from jax.experimental.pallas import tpu as pltpu
from jax.sharding import PartitionSpec as P

RG_DEV = 8
HIGH = lax.Precision.HIGHEST
NT = (((1,), (1,)), ((), ()))
MESH = pl.DeviceIdType.MESH


def lag_kernel(sel_ref, x_ref, y_ref, o_ref):
    width = x_ref.shape[3]
    for a in range(2):
        xre = x_ref[0, 0, a]
        xim = x_ref[0, 1, a]
        for b in range(2):
            yre = y_ref[0, 0, b]
            yim = y_ref[0, 1, b]
            dot = lambda u, v: lax.dot_general(u, v, NT, preferred_element_type=jnp.float32)
            real_part = dot(xre, yre) + dot(xim, yim)
            imag_part = dot(xim, yre) - dot(xre, yim)
            for c, part in enumerate((real_part, imag_part)):
                padded = jnp.concatenate([part, jnp.zeros_like(part)], axis=1)
                sheared = pltpu.roll(padded, 0, 1, stride=1, stride_axis=0)
                row = (a * 2 + b) * 2 + c
                o_ref[0, pl.ds(row, 1), :] = jnp.sum(sheared, axis=0, keepdims=True)
    del width


def pair_lags(sel, x_all, y_all, y_by_sel):
    n = sel.shape[0]
    _, _, _, width, samples = x_all.shape
    x_spec = pl.BlockSpec((1, 2, 2, width, samples), lambda i, s: (s[i], 0, 0, 0, 0))
    if y_by_sel:
        y_spec = pl.BlockSpec((1, 2, 2, width, samples), lambda i, s: (s[i], 0, 0, 0, 0))
    else:
        y_spec = pl.BlockSpec((1, 2, 2, width, samples), lambda i, s: (i, 0, 0, 0, 0))
    out_spec = pl.BlockSpec((1, 8, 2 * width), lambda i, s: (i, 0, 0))
    flops = n * 16 * 2 * width * width * samples
    return pl.pallas_call(
        lag_kernel,
        out_shape=jax.ShapeDtypeStruct((n, 8, 2 * width), jnp.float32),
        grid_spec=pltpu.PrefetchScalarGridSpec(
            num_scalar_prefetch=1,
            grid=(n,),
            in_specs=[x_spec, y_spec],
            out_specs=out_spec,
        ),
        compiler_params=pltpu.CompilerParams(vmem_limit_bytes=48 * 1024 * 1024),
        cost_estimate=pl.CostEstimate(
            flops=flops, transcendentals=0, bytes_accessed=n * 2 * 4 * width * samples * 2
        ),
    )(sel, x_all, y_all)


def scatter_kernel(dense_ref, out_ref, recv, send_sem, recv_sem):
    n = dense_ref.shape[0]
    me = lax.axis_index("inp")
    fq = lax.axis_index("freq")
    barrier = pltpu.get_barrier_semaphore()
    for o in range(1, n):
        pl.semaphore_signal(barrier, inc=1, device_id=(lax.rem(me + o, n), fq), device_id_type=MESH)
    pl.semaphore_wait(barrier, n - 1)
    copies = []
    for o in range(1, n):
        target = lax.rem(me + o, n)
        copy = pltpu.make_async_remote_copy(
            src_ref=dense_ref.at[target],
            dst_ref=recv.at[o - 1],
            send_sem=send_sem.at[o - 1],
            recv_sem=recv_sem.at[o - 1],
            device_id=(target, fq),
            device_id_type=MESH,
        )
        copy.start()
        copies.append(copy)
    for copy in copies:
        copy.wait()
    total = dense_ref[me]
    for o in range(n - 1):
        total = total + recv[o]
    out_ref[...] = total


def reduce_scatter(dense):
    n = dense.shape[0]
    slab = dense.shape[1:]
    return pl.pallas_call(
        scatter_kernel,
        out_shape=jax.ShapeDtypeStruct(slab, jnp.float32),
        in_specs=[pl.BlockSpec(memory_space=pltpu.VMEM)],
        out_specs=pl.BlockSpec(memory_space=pltpu.VMEM),
        scratch_shapes=[
            pltpu.VMEM((n - 1,) + slab, jnp.float32),
            pltpu.SemaphoreType.DMA((n - 1,)),
            pltpu.SemaphoreType.DMA((n - 1,)),
        ],
        compiler_params=pltpu.CompilerParams(collective_id=0, has_side_effects=True),
    )(dense)


def on_device(volts, position_input, tile_group):
    blocks, width = position_input.shape
    channels, _, _, samples = volts.shape
    diffs = 2 * width - 1
    n_inp = lax.axis_size("inp")
    levels = n_inp.bit_length() - 1
    me = lax.axis_index("inp")

    sent = []
    for bit in range(levels):
        mine = (me >> bit) & 1
        pairs = [(i, i ^ (1 << bit)) for i in range(n_inp)]
        send = lax.dynamic_index_in_dim(volts, 1 - mine, axis=0, keepdims=True)
        got = lax.ppermute(send, "inp", pairs)
        got_pos = lax.ppermute(position_input, "inp", pairs)
        got_tg = lax.ppermute(tile_group, "inp", pairs)
        sent.append((mine, got, got_pos, got_tg))

    ids = jnp.arange(width, dtype=jnp.int32)

    def reorder(pos, raw, reverse):
        perm = (pos[:, :, None] == ids[None, None, :]).astype(raw.dtype)
        if reverse:
            perm = perm[:, ::-1, :]
        r5 = raw.reshape(raw.shape[0], 2, blocks, width, samples)
        return jnp.einsum("api,fcais->fcaps", perm, r5, preferred_element_type=jnp.float32).astype(raw.dtype)

    ordered = reorder(position_input, volts, False)
    reversed_ = reorder(position_input, volts, True)

    groups_all = RG_DEV * n_inp
    group_ids = jnp.arange(groups_all, dtype=jnp.int32)

    lag0 = pair_lags(jnp.arange(channels, dtype=jnp.int32), ordered, reversed_, True)
    lag0 = lag0.reshape(channels, 2, 2, 2, 2 * width)
    center = (jnp.arange(2 * width) == width - 1)
    same = jnp.eye(2, dtype=bool)
    lag0 = jnp.where(same[None, :, :, None, None] & center[None, None, None, None, :], 0.0, lag0)
    w0 = (tile_group[:, 0, :, None] == group_ids).astype(jnp.float32)
    dense_rev = jnp.einsum("abg,fabcj->gfcj", w0, lag0, precision=HIGH)
    dense_fwd = None
    chan_ids = jnp.arange(channels, dtype=jnp.int32)
    sign = jnp.array([1.0, -1.0], jnp.float32)
    for bit in range(levels):
        mine, got, got_pos, got_tg = sent[bit]
        partner_rev = reorder(got_pos, got, True)
        lag = pair_lags(mine[None].astype(jnp.int32), ordered, partner_rev, False)
        lag = lag.reshape(2, 2, 2, 2 * width)
        fmask = (chan_ids == mine).astype(jnp.float32)
        w_direct = (tile_group[:, bit + 1, :, None] == group_ids).astype(jnp.float32)
        w_trans = (got_tg[:, bit + 1, :, None] == group_ids).astype(jnp.float32)
        dense_rev = dense_rev + jnp.einsum("abg,f,abcj->gfcj", w_direct, fmask, lag, precision=HIGH)
        term = jnp.einsum("bag,f,c,abcj->gfcj", w_trans, fmask, sign, lag, precision=HIGH)
        dense_fwd = term if dense_fwd is None else dense_fwd + term
    dense = jnp.flip(dense_rev[..., :diffs], axis=-1) + dense_fwd[..., :diffs]
    dense = dense * (1.0 / samples)
    dense = jnp.pad(dense, [(0, 0)] * 3 + [(0, 1)])
    dense = dense.reshape((n_inp, RG_DEV) + dense.shape[1:])
    return reduce_scatter(dense)[..., :diffs]


def solution(mesh):
    return jax.shard_map(
        on_device,
        mesh=mesh,
        in_specs=(P("freq", None, "inp", None), P("inp", None), P("inp", None, None)),
        out_specs=P("inp", "freq", None, None),
        check_vma=False,
    )
```

```python
import jax
import jax.numpy as jnp
from jax import lax
from jax.experimental import pallas as pl
from jax.experimental.pallas import tpu as pltpu
from jax.sharding import PartitionSpec as P

RG_DEV = 8
HIGH = lax.Precision.HIGHEST
NT = (((1,), (1,)), ((), ()))
MESH = pl.DeviceIdType.MESH


def lag_kernel(sel_ref, xraw_ref, xperm_ref, yraw_ref, yperm_ref, o_ref, xs, ys):
    width = xperm_ref.shape[1]
    for blk in range(2):
        for c in range(2):
            rows = pl.ds(blk * width, width)
            xs[blk, c] = jnp.dot(
                xperm_ref[blk], xraw_ref[0, c, rows, :], preferred_element_type=jnp.float32
            ).astype(xs.dtype)
            ys[blk, c] = jnp.dot(
                yperm_ref[blk], yraw_ref[0, c, rows, :], preferred_element_type=jnp.float32
            ).astype(ys.dtype)
    dot = lambda u, v: lax.dot_general(u, v, NT, preferred_element_type=jnp.float32)
    for a in range(2):
        xre = xs[a, 0]
        xim = xs[a, 1]
        for b in range(2):
            yre = ys[b, 0]
            yim = ys[b, 1]
            real_part = dot(xre, yre) + dot(xim, yim)
            imag_part = dot(xim, yre) - dot(xre, yim)
            for c, part in enumerate((real_part, imag_part)):
                padded = jnp.concatenate([part, jnp.zeros_like(part)], axis=1)
                sheared = pltpu.roll(padded, 0, 1, stride=1, stride_axis=0)
                row = (a * 2 + b) * 2 + c
                o_ref[0, pl.ds(row, 1), :] = jnp.sum(sheared, axis=0, keepdims=True)


def pair_lags(sel, x_raw, x_perm, y_raw, y_perm, y_by_sel):
    n = sel.shape[0]
    _, _, rows_x, samples = x_raw.shape
    rows_y = y_raw.shape[2]
    width = x_perm.shape[1]
    x_spec = pl.BlockSpec((1, 2, rows_x, samples), lambda i, s: (s[i], 0, 0, 0))
    if y_by_sel:
        y_spec = pl.BlockSpec((1, 2, rows_y, samples), lambda i, s: (s[i], 0, 0, 0))
    else:
        y_spec = pl.BlockSpec((1, 2, rows_y, samples), lambda i, s: (i, 0, 0, 0))
    perm_spec = pl.BlockSpec((2, width, width), lambda i, s: (0, 0, 0))
    out_spec = pl.BlockSpec((1, 8, 2 * width), lambda i, s: (i, 0, 0))
    flops = n * (16 + 8) * 2 * width * width * samples
    return pl.pallas_call(
        lag_kernel,
        out_shape=jax.ShapeDtypeStruct((n, 8, 2 * width), jnp.float32),
        grid_spec=pltpu.PrefetchScalarGridSpec(
            num_scalar_prefetch=1,
            grid=(n,),
            in_specs=[x_spec, perm_spec, y_spec, perm_spec],
            out_specs=out_spec,
            scratch_shapes=[
                pltpu.VMEM((2, 2, width, samples), x_raw.dtype),
                pltpu.VMEM((2, 2, width, samples), x_raw.dtype),
            ],
        ),
        compiler_params=pltpu.CompilerParams(vmem_limit_bytes=48 * 1024 * 1024),
        cost_estimate=pl.CostEstimate(
            flops=flops, transcendentals=0, bytes_accessed=n * 2 * 4 * width * samples * 2
        ),
    )(sel, x_raw, x_perm, y_raw, y_perm)


def scatter_kernel(dense_ref, out_ref, recv, send_sem, recv_sem):
    n = dense_ref.shape[0]
    me = lax.axis_index("inp")
    fq = lax.axis_index("freq")
    barrier = pltpu.get_barrier_semaphore()
    for o in range(1, n):
        pl.semaphore_signal(barrier, inc=1, device_id=(lax.rem(me + o, n), fq), device_id_type=MESH)
    pl.semaphore_wait(barrier, n - 1)
    copies = []
    for o in range(1, n):
        target = lax.rem(me + o, n)
        copy = pltpu.make_async_remote_copy(
            src_ref=dense_ref.at[target],
            dst_ref=recv.at[o - 1],
            send_sem=send_sem.at[o - 1],
            recv_sem=recv_sem.at[o - 1],
            device_id=(target, fq),
            device_id_type=MESH,
        )
        copy.start()
        copies.append(copy)
    for copy in copies:
        copy.wait()
    total = dense_ref[me]
    for o in range(n - 1):
        total = total + recv[o]
    out_ref[...] = total


def reduce_scatter(dense):
    n = dense.shape[0]
    slab = dense.shape[1:]
    return pl.pallas_call(
        scatter_kernel,
        out_shape=jax.ShapeDtypeStruct(slab, jnp.float32),
        in_specs=[pl.BlockSpec(memory_space=pltpu.VMEM)],
        out_specs=pl.BlockSpec(memory_space=pltpu.VMEM),
        scratch_shapes=[
            pltpu.VMEM((n - 1,) + slab, jnp.float32),
            pltpu.SemaphoreType.DMA((n - 1,)),
            pltpu.SemaphoreType.DMA((n - 1,)),
        ],
        compiler_params=pltpu.CompilerParams(collective_id=0, has_side_effects=True),
    )(dense)


def on_device(volts, position_input, tile_group):
    blocks, width = position_input.shape
    channels, _, rows, samples = volts.shape
    diffs = 2 * width - 1
    n_inp = lax.axis_size("inp")
    levels = n_inp.bit_length() - 1
    me = lax.axis_index("inp")

    pos_row = jnp.pad(position_input.reshape(-1), (0, samples - blocks * width))
    tg_flat = tile_group.reshape(-1)
    tg_row = jnp.pad(tg_flat, (0, samples - tg_flat.shape[0]))
    meta = jnp.zeros((2, 16, samples), jnp.float32)
    meta = meta.at[0, 0].set(pos_row.astype(jnp.float32)).at[0, 1].set(tg_row.astype(jnp.float32))
    meta = meta.astype(volts.dtype)

    sent = []
    for bit in range(levels):
        mine = (me >> bit) & 1
        pairs = [(i, i ^ (1 << bit)) for i in range(n_inp)]
        chan = jnp.where(mine == 1, volts[0], volts[1])
        send = jnp.concatenate([chan, meta], axis=1)[None]
        got = lax.ppermute(send, "inp", pairs)
        sent.append((mine, got))

    ids = jnp.arange(width, dtype=jnp.int32)

    def one_hot(pos, reverse):
        if reverse:
            pos = pos[:, ::-1]
        return (pos[:, :, None] == ids[None, None, :]).astype(volts.dtype)

    perm = one_hot(position_input, False)
    perm_rev = one_hot(position_input, True)

    groups_all = RG_DEV * n_inp
    group_ids = jnp.arange(groups_all, dtype=jnp.int32)

    lag0 = pair_lags(jnp.arange(channels, dtype=jnp.int32), volts, perm, volts, perm_rev, True)
    lag0 = lag0.reshape(channels, 2, 2, 2, 2 * width)
    center = (jnp.arange(2 * width) == width - 1)
    same = jnp.eye(2, dtype=bool)
    lag0 = jnp.where(same[None, :, :, None, None] & center[None, None, None, None, :], 0.0, lag0)
    w0 = (tile_group[:, 0, :, None] == group_ids).astype(jnp.float32)
    dense_rev = jnp.einsum("abg,fabcj->gfcj", w0, lag0, precision=HIGH)
    dense_fwd = None
    chan_ids = jnp.arange(channels, dtype=jnp.int32)
    sign = jnp.array([1.0, -1.0], jnp.float32)
    for bit in range(levels):
        mine, got = sent[bit]
        got_pos = got[0, 0, rows, : blocks * width].astype(jnp.int32).reshape(blocks, width)
        got_tg = got[0, 0, rows + 1, : tg_flat.shape[0]].astype(jnp.int32).reshape(tile_group.shape)
        lag = pair_lags(mine[None].astype(jnp.int32), volts, perm, got, one_hot(got_pos, True), False)
        lag = lag.reshape(2, 2, 2, 2 * width)
        fmask = (chan_ids == mine).astype(jnp.float32)
        w_direct = (tile_group[:, bit + 1, :, None] == group_ids).astype(jnp.float32)
        w_trans = (got_tg[:, bit + 1, :, None] == group_ids).astype(jnp.float32)
        dense_rev = dense_rev + jnp.einsum("abg,f,abcj->gfcj", w_direct, fmask, lag, precision=HIGH)
        term = jnp.einsum("bag,f,c,abcj->gfcj", w_trans, fmask, sign, lag, precision=HIGH)
        dense_fwd = term if dense_fwd is None else dense_fwd + term
    dense = jnp.flip(dense_rev[..., :diffs], axis=-1) + dense_fwd[..., :diffs]
    dense = dense * (1.0 / samples)
    dense = jnp.pad(dense, [(0, 0)] * 3 + [(0, 1)])
    dense = dense.reshape((n_inp, RG_DEV) + dense.shape[1:])
    return reduce_scatter(dense)[..., :diffs]


def solution(mesh):
    return jax.shard_map(
        on_device,
        mesh=mesh,
        in_specs=(P("freq", None, "inp", None), P("inp", None), P("inp", None, None)),
        out_specs=P("inp", "freq", None, None),
        check_vma=False,
    )
```

```python
import jax
import jax.numpy as jnp
from jax import lax
from jax.experimental import pallas as pl
from jax.experimental.pallas import tpu as pltpu
from jax.sharding import PartitionSpec as P

RG_DEV = 8
HIGH = lax.Precision.HIGHEST
NT = (((1,), (1,)), ((), ()))
MESH = pl.DeviceIdType.MESH


def lag_kernel(sel_ref, xraw_ref, xperm_ref, yre_ref, yim_ref, yperm_ref, o_ref, xs, ys):
    width = xperm_ref.shape[1]
    for blk in range(2):
        rows = pl.ds(blk * width, width)
        for c, y_ref in enumerate((yre_ref, yim_ref)):
            xs[blk, c] = jnp.dot(
                xperm_ref[blk], xraw_ref[0, c, rows, :], preferred_element_type=jnp.float32
            ).astype(xs.dtype)
            ys[blk, c] = jnp.dot(
                yperm_ref[blk], y_ref[0, 0, rows, :], preferred_element_type=jnp.float32
            ).astype(ys.dtype)
    dot = lambda u, v: lax.dot_general(u, v, NT, preferred_element_type=jnp.float32)
    for a in range(2):
        xre = xs[a, 0]
        xim = xs[a, 1]
        for b in range(2):
            yre = ys[b, 0]
            yim = ys[b, 1]
            real_part = dot(xre, yre) + dot(xim, yim)
            imag_part = dot(xim, yre) - dot(xre, yim)
            for c, part in enumerate((real_part, imag_part)):
                padded = jnp.concatenate([part, jnp.zeros_like(part)], axis=1)
                sheared = pltpu.roll(padded, 0, 1, stride=1, stride_axis=0)
                row = (a * 2 + b) * 2 + c
                o_ref[0, pl.ds(row, 1), :] = jnp.sum(sheared, axis=0, keepdims=True)


def pair_lags(sel, x_raw, x_perm, y_re, y_im, y_perm, y_by_sel):
    n = sel.shape[0]
    _, _, rows_x, samples = x_raw.shape
    rows_y = y_re.shape[2]
    width = x_perm.shape[1]
    x_spec = pl.BlockSpec((1, 2, rows_x, samples), lambda i, s: (s[i], 0, 0, 0))
    if y_by_sel:
        re_spec = pl.BlockSpec((1, 1, rows_y, samples), lambda i, s: (s[i], 0, 0, 0))
        im_spec = pl.BlockSpec((1, 1, rows_y, samples), lambda i, s: (s[i], 1, 0, 0))
    else:
        re_spec = pl.BlockSpec((1, 1, rows_y, samples), lambda i, s: (i, 0, 0, 0))
        im_spec = pl.BlockSpec((1, 1, rows_y, samples), lambda i, s: (i, 0, 0, 0))
    perm_spec = pl.BlockSpec((2, width, width), lambda i, s: (0, 0, 0))
    out_spec = pl.BlockSpec((1, 8, 2 * width), lambda i, s: (i, 0, 0))
    flops = n * (16 + 8) * 2 * width * width * samples
    return pl.pallas_call(
        lag_kernel,
        out_shape=jax.ShapeDtypeStruct((n, 8, 2 * width), jnp.float32),
        grid_spec=pltpu.PrefetchScalarGridSpec(
            num_scalar_prefetch=1,
            grid=(n,),
            in_specs=[x_spec, perm_spec, re_spec, im_spec, perm_spec],
            out_specs=out_spec,
            scratch_shapes=[
                pltpu.VMEM((2, 2, width, samples), x_raw.dtype),
                pltpu.VMEM((2, 2, width, samples), x_raw.dtype),
            ],
        ),
        compiler_params=pltpu.CompilerParams(vmem_limit_bytes=48 * 1024 * 1024),
        cost_estimate=pl.CostEstimate(
            flops=flops, transcendentals=0, bytes_accessed=n * 2 * 4 * width * samples * 2
        ),
    )(sel, x_raw, x_perm, y_re, y_im, y_perm)


def scatter_kernel(dense_ref, out_ref, recv, send_sem, recv_sem):
    n = dense_ref.shape[0]
    me = lax.axis_index("inp")
    fq = lax.axis_index("freq")
    barrier = pltpu.get_barrier_semaphore()
    for o in range(1, n):
        pl.semaphore_signal(barrier, inc=1, device_id=(lax.rem(me + o, n), fq), device_id_type=MESH)
    pl.semaphore_wait(barrier, n - 1)
    copies = []
    for o in range(1, n):
        target = lax.rem(me + o, n)
        copy = pltpu.make_async_remote_copy(
            src_ref=dense_ref.at[target],
            dst_ref=recv.at[o - 1],
            send_sem=send_sem.at[o - 1],
            recv_sem=recv_sem.at[o - 1],
            device_id=(target, fq),
            device_id_type=MESH,
        )
        copy.start()
        copies.append(copy)
    for copy in copies:
        copy.wait()
    total = dense_ref[me]
    for o in range(n - 1):
        total = total + recv[o]
    out_ref[...] = total


def reduce_scatter(dense):
    n = dense.shape[0]
    slab = dense.shape[1:]
    return pl.pallas_call(
        scatter_kernel,
        out_shape=jax.ShapeDtypeStruct(slab, jnp.float32),
        in_specs=[pl.BlockSpec(memory_space=pltpu.VMEM)],
        out_specs=pl.BlockSpec(memory_space=pltpu.VMEM),
        scratch_shapes=[
            pltpu.VMEM((n - 1,) + slab, jnp.float32),
            pltpu.SemaphoreType.DMA((n - 1,)),
            pltpu.SemaphoreType.DMA((n - 1,)),
        ],
        compiler_params=pltpu.CompilerParams(collective_id=0, has_side_effects=True),
    )(dense)


def on_device(volts, position_input, tile_group):
    blocks, width = position_input.shape
    channels, _, rows, samples = volts.shape
    diffs = 2 * width - 1
    n_inp = lax.axis_size("inp")
    levels = n_inp.bit_length() - 1
    me = lax.axis_index("inp")

    pos_row = jnp.pad(position_input.reshape(-1), (0, samples - blocks * width))
    tg_flat = tile_group.reshape(-1)
    tg_row = jnp.pad(tg_flat, (0, samples - tg_flat.shape[0]))
    meta = jnp.zeros((2, 16, samples), jnp.float32)
    meta = meta.at[0, 0].set(pos_row.astype(jnp.float32)).at[0, 1].set(tg_row.astype(jnp.float32))
    meta = meta.astype(volts.dtype)

    def exchange(chan, pairs):
        slab = jnp.concatenate([jnp.where(chan == 1, volts[1], volts[0]), meta], axis=1)
        return [lax.ppermute(slab[None, c : c + 1], "inp", pairs) for c in range(2)]

    mine = [me & 1] + [((me >> 1) ^ (me >> 2)) & 1] * min(levels - 1, 2)
    mine += [(me >> bit) & 1 for bit in range(3, levels)]
    got = {}
    got[1] = exchange(1 - mine[1], [(i, i ^ 2) for i in range(n_inp)]) if levels > 1 else None
    got[0] = exchange(1 - mine[0], [(i, i ^ 1) for i in range(n_inp)])
    relay = [(i, i ^ 6) for i in range(n_inp)]
    for bit in range(2, levels):
        if bit == 2:
            got[2] = [lax.ppermute(part, "inp", relay) for part in got[1]]
        else:
            got[bit] = exchange(1 - mine[bit], [(i, i ^ (1 << bit)) for i in range(n_inp)])

    ids = jnp.arange(width, dtype=jnp.int32)

    def one_hot(pos, reverse):
        if reverse:
            pos = pos[:, ::-1]
        return (pos[:, :, None] == ids[None, None, :]).astype(volts.dtype)

    perm = one_hot(position_input, False)
    perm_rev = one_hot(position_input, True)

    groups_all = RG_DEV * n_inp
    group_ids = jnp.arange(groups_all, dtype=jnp.int32)
    chan_ids = jnp.arange(channels, dtype=jnp.int32)

    lag0 = pair_lags(jnp.arange(channels, dtype=jnp.int32), volts, perm, volts, volts, perm_rev, True)
    lag0 = lag0.reshape(channels, 2, 2, 2, 2 * width)
    center = (jnp.arange(2 * width) == width - 1)
    same = jnp.eye(2, dtype=bool)
    lag0 = jnp.where(same[None, :, :, None, None] & center[None, None, None, None, :], 0.0, lag0)
    contrib_w = []
    contrib_v = []
    w0 = (tile_group[:, 0, :, None] == group_ids).astype(jnp.float32)
    f0 = (chan_ids[:, None] == chan_ids[None, :]).astype(jnp.float32)
    contrib_w.append(jnp.einsum("abg,fh->fabgh", w0, f0).reshape(-1, groups_all, channels))
    contrib_v.append(jnp.flip(lag0[..., :diffs], axis=-1).reshape(-1, 2, diffs))
    sign = jnp.array([1.0, -1.0], jnp.float32)
    for bit in range(levels):
        yre, yim = got[bit]
        got_pos = yre[0, 0, rows, : blocks * width].astype(jnp.int32).reshape(blocks, width)
        got_tg = yre[0, 0, rows + 1, : tg_flat.shape[0]].astype(jnp.int32).reshape(tile_group.shape)
        lag = pair_lags(mine[bit][None].astype(jnp.int32), volts, perm, yre, yim, one_hot(got_pos, True), False)
        lag = lag.reshape(2, 2, 2, 2 * width)[..., :diffs]
        fmask = (chan_ids == mine[bit]).astype(jnp.float32)
        w_direct = (tile_group[:, bit + 1, :, None] == group_ids).astype(jnp.float32)
        w_trans = jnp.swapaxes((got_tg[:, bit + 1, :, None] == group_ids).astype(jnp.float32), 0, 1)
        contrib_w.append(jnp.einsum("abg,f->abgf", w_direct, fmask).reshape(-1, groups_all, channels))
        contrib_v.append(jnp.flip(lag, axis=-1).reshape(-1, 2, diffs))
        contrib_w.append(jnp.einsum("abg,f->abgf", w_trans, fmask).reshape(-1, groups_all, channels))
        contrib_v.append((lag * sign[:, None]).reshape(-1, 2, diffs))
    dense = jnp.einsum(
        "ngf,nck->gfck", jnp.concatenate(contrib_w), jnp.concatenate(contrib_v), precision=HIGH
    )
    dense = dense * (1.0 / samples)
    dense = jnp.pad(dense, [(0, 0)] * 3 + [(0, 1)])
    dense = dense.reshape((n_inp, RG_DEV) + dense.shape[1:])
    return reduce_scatter(dense)[..., :diffs]


def solution(mesh):
    return jax.shard_map(
        on_device,
        mesh=mesh,
        in_specs=(P("freq", None, "inp", None), P("inp", None), P("inp", None, None)),
        out_specs=P("inp", "freq", None, None),
        check_vma=False,
    )
```

```python
import jax
import jax.numpy as jnp
from jax import lax
from jax.experimental import pallas as pl
from jax.experimental.pallas import tpu as pltpu
from jax.sharding import PartitionSpec as P

RG_DEV = 8
HIGH = lax.Precision.HIGHEST
NT = (((1,), (1,)), ((), ()))
MESH = pl.DeviceIdType.MESH


def lags_into(x_ref, chan, xperm_ref, yre_ref, yim_ref, yperm_ref, o_ref, slot, xs, ys):
    width = xperm_ref.shape[1]
    for blk in range(2):
        rows = pl.ds(blk * width, width)
        for c, y_ref in enumerate((yre_ref, yim_ref)):
            xs[blk, c] = jnp.dot(
                xperm_ref[blk], x_ref[chan, c, rows, :], preferred_element_type=jnp.float32
            ).astype(xs.dtype)
            ys[blk, c] = jnp.dot(
                yperm_ref[blk], y_ref[0, 0, rows, :], preferred_element_type=jnp.float32
            ).astype(ys.dtype)
    dot = lambda u, v: lax.dot_general(u, v, NT, preferred_element_type=jnp.float32)
    for a in range(2):
        xre = xs[a, 0]
        xim = xs[a, 1]
        for b in range(2):
            yre = ys[b, 0]
            yim = ys[b, 1]
            real_part = dot(xre, yre) + dot(xim, yim)
            imag_part = dot(xim, yre) - dot(xre, yim)
            for c, part in enumerate((real_part, imag_part)):
                padded = jnp.concatenate([part, jnp.zeros_like(part)], axis=1)
                sheared = pltpu.roll(padded, 0, 1, stride=1, stride_axis=0)
                row = (a * 2 + b) * 2 + c
                o_ref[slot, pl.ds(row, 1), :] = jnp.sum(sheared, axis=0, keepdims=True)


def lag_kernel(sel_ref, xraw_ref, xperm_ref, yre_ref, yim_ref, yperm_ref, o_ref, xs, ys):
    lags_into(xraw_ref, 0, xperm_ref, yre_ref, yim_ref, yperm_ref, o_ref, 0, xs, ys)


def relay_kernel(x_ref, xperm_ref, yre_ref, yim_ref, yperm_ref, z_ref, zperm_ref,
                 o_ref, relay_ref, xs, ys, send_sem, recv_sem):
    me = lax.axis_index("inp")
    fq = lax.axis_index("freq")
    onward = lax.bitwise_xor(me, 6)
    barrier = pltpu.get_barrier_semaphore()
    pl.semaphore_signal(barrier, inc=1, device_id=(onward, fq), device_id_type=MESH)
    pl.semaphore_wait(barrier, 1)
    copy = pltpu.make_async_remote_copy(
        src_ref=yim_ref,
        dst_ref=relay_ref,
        send_sem=send_sem,
        recv_sem=recv_sem,
        device_id=(onward, fq),
        device_id_type=MESH,
    )
    copy.start()
    parity = lax.bitwise_and(lax.bitwise_xor(lax.shift_right_logical(me, 1), lax.shift_right_logical(me, 2)), 1)
    lags_into(x_ref, parity, xperm_ref, yre_ref, yim_ref, yperm_ref, o_ref, 0, xs, ys)
    lags_into(x_ref, lax.bitwise_and(me, 1), xperm_ref, z_ref.at[:, 0:1], z_ref.at[:, 1:2], zperm_ref, o_ref, 1, xs, ys)
    copy.wait()


def relay_lags(x_all, x_perm, y_re, y_im, y_perm, z_all, z_perm):
    width = x_perm.shape[1]
    samples = x_all.shape[-1]
    vmem = pl.BlockSpec(memory_space=pltpu.VMEM)
    return pl.pallas_call(
        relay_kernel,
        out_shape=(
            jax.ShapeDtypeStruct((2, 8, 2 * width), jnp.float32),
            jax.ShapeDtypeStruct(y_im.shape, y_im.dtype),
        ),
        in_specs=[vmem] * 7,
        out_specs=(vmem, vmem),
        scratch_shapes=[
            pltpu.VMEM((2, 2, width, samples), x_all.dtype),
            pltpu.VMEM((2, 2, width, samples), x_all.dtype),
            pltpu.SemaphoreType.DMA(()),
            pltpu.SemaphoreType.DMA(()),
        ],
        compiler_params=pltpu.CompilerParams(
            collective_id=1, has_side_effects=True, vmem_limit_bytes=48 * 1024 * 1024
        ),
        cost_estimate=pl.CostEstimate(
            flops=2 * 4 * 24 * 2 * width * width * samples, transcendentals=0,
            bytes_accessed=4 * 2 * 4 * width * samples * 2,
        ),
    )(x_all, x_perm, y_re, y_im, y_perm, z_all, z_perm)


def pair_lags(sel, x_raw, x_perm, y_re, y_im, y_perm, y_by_sel):
    n = sel.shape[0]
    _, _, rows_x, samples = x_raw.shape
    rows_y = y_re.shape[2]
    width = x_perm.shape[1]
    x_spec = pl.BlockSpec((1, 2, rows_x, samples), lambda i, s: (s[i], 0, 0, 0))
    if y_by_sel:
        re_spec = pl.BlockSpec((1, 1, rows_y, samples), lambda i, s: (s[i], 0, 0, 0))
        im_spec = pl.BlockSpec((1, 1, rows_y, samples), lambda i, s: (s[i], 1, 0, 0))
    else:
        re_spec = pl.BlockSpec((1, 1, rows_y, samples), lambda i, s: (i, 0, 0, 0))
        im_spec = pl.BlockSpec((1, 1, rows_y, samples), lambda i, s: (i, 0, 0, 0))
    perm_spec = pl.BlockSpec((2, width, width), lambda i, s: (0, 0, 0))
    out_spec = pl.BlockSpec((1, 8, 2 * width), lambda i, s: (i, 0, 0))
    flops = n * (16 + 8) * 2 * width * width * samples
    return pl.pallas_call(
        lag_kernel,
        out_shape=jax.ShapeDtypeStruct((n, 8, 2 * width), jnp.float32),
        grid_spec=pltpu.PrefetchScalarGridSpec(
            num_scalar_prefetch=1,
            grid=(n,),
            in_specs=[x_spec, perm_spec, re_spec, im_spec, perm_spec],
            out_specs=out_spec,
            scratch_shapes=[
                pltpu.VMEM((2, 2, width, samples), x_raw.dtype),
                pltpu.VMEM((2, 2, width, samples), x_raw.dtype),
            ],
        ),
        compiler_params=pltpu.CompilerParams(vmem_limit_bytes=48 * 1024 * 1024),
        cost_estimate=pl.CostEstimate(
            flops=flops, transcendentals=0, bytes_accessed=n * 2 * 4 * width * samples * 2
        ),
    )(sel, x_raw, x_perm, y_re, y_im, y_perm)


def scatter_kernel(dense_ref, out_ref, recv, send_sem, recv_sem):
    n = dense_ref.shape[0]
    me = lax.axis_index("inp")
    fq = lax.axis_index("freq")
    barrier = pltpu.get_barrier_semaphore()
    for o in range(1, n):
        pl.semaphore_signal(barrier, inc=1, device_id=(lax.rem(me + o, n), fq), device_id_type=MESH)
    pl.semaphore_wait(barrier, n - 1)
    copies = []
    for o in range(1, n):
        target = lax.rem(me + o, n)
        copy = pltpu.make_async_remote_copy(
            src_ref=dense_ref.at[target],
            dst_ref=recv.at[o - 1],
            send_sem=send_sem.at[o - 1],
            recv_sem=recv_sem.at[o - 1],
            device_id=(target, fq),
            device_id_type=MESH,
        )
        copy.start()
        copies.append(copy)
    for copy in copies:
        copy.wait()
    total = dense_ref[me]
    for o in range(n - 1):
        total = total + recv[o]
    out_ref[...] = total


def reduce_scatter(dense):
    n = dense.shape[0]
    slab = dense.shape[1:]
    return pl.pallas_call(
        scatter_kernel,
        out_shape=jax.ShapeDtypeStruct(slab, jnp.float32),
        in_specs=[pl.BlockSpec(memory_space=pltpu.VMEM)],
        out_specs=pl.BlockSpec(memory_space=pltpu.VMEM),
        scratch_shapes=[
            pltpu.VMEM((n - 1,) + slab, jnp.float32),
            pltpu.SemaphoreType.DMA((n - 1,)),
            pltpu.SemaphoreType.DMA((n - 1,)),
        ],
        compiler_params=pltpu.CompilerParams(collective_id=0, has_side_effects=True),
    )(dense)


def on_device(volts, position_input, tile_group):
    blocks, width = position_input.shape
    channels, _, rows, samples = volts.shape
    diffs = 2 * width - 1
    n_inp = lax.axis_size("inp")
    levels = n_inp.bit_length() - 1
    me = lax.axis_index("inp")

    pos_row = jnp.pad(position_input.reshape(-1), (0, samples - blocks * width))
    tg_flat = tile_group.reshape(-1)
    tg_row = jnp.pad(tg_flat, (0, samples - tg_flat.shape[0]))
    meta = jnp.stack([pos_row, tg_row]).astype(jnp.float32).astype(volts.dtype)
    meta = jnp.pad(meta[None], [(0, 1), (0, 14), (0, 0)])

    def exchange(chan, pairs, parts):
        slab = jnp.concatenate([jnp.where(chan == 1, volts[1], volts[0]), meta], axis=1)
        if parts == 1:
            got_slab = lax.ppermute(slab[None], "inp", pairs)
            return [got_slab[:, c : c + 1] for c in range(2)]
        return [lax.ppermute(slab[None, c : c + 1], "inp", pairs) for c in range(2)]

    mine = [me & 1] + [((me >> 1) ^ (me >> 2)) & 1] * min(levels - 1, 2)
    mine += [(me >> bit) & 1 for bit in range(3, levels)]
    got1 = exchange(1 - mine[1], [(i, i ^ 2) for i in range(n_inp)], 2)
    got0 = lax.ppermute(
        jnp.concatenate([jnp.where(mine[0] == 0, volts[1], volts[0]), meta], axis=1)[None],
        "inp",
        [(i, i ^ 1) for i in range(n_inp)],
    )
    relay_re = lax.ppermute(got1[0], "inp", [(i, i ^ 6) for i in range(n_inp)])

    ids = jnp.arange(width, dtype=jnp.int32)

    def one_hot(pos, reverse):
        if reverse:
            pos = pos[:, ::-1]
        return (pos[:, :, None] == ids[None, None, :]).astype(volts.dtype)

    perm = one_hot(position_input, False)
    perm_rev = one_hot(position_input, True)

    groups_all = RG_DEV * n_inp
    group_ids = jnp.arange(groups_all, dtype=jnp.int32)
    chan_ids = jnp.arange(channels, dtype=jnp.int32)

    lag0 = pair_lags(jnp.arange(channels, dtype=jnp.int32), volts, perm, volts, volts, perm_rev, True)
    lag0 = lag0.reshape(channels, 2, 2, 2, 2 * width)
    center = (jnp.arange(2 * width) == width - 1)
    same = jnp.eye(2, dtype=bool)
    lag0 = jnp.where(same[None, :, :, None, None] & center[None, None, None, None, :], 0.0, lag0)
    contrib_w = []
    contrib_v = []
    w0 = (tile_group[:, 0, :, None] == group_ids).astype(jnp.float32)
    f0 = (chan_ids[:, None] == chan_ids[None, :]).astype(jnp.float32)
    contrib_w.append(jnp.einsum("abg,fh->fabgh", w0, f0).reshape(-1, groups_all, channels))
    contrib_v.append(jnp.flip(lag0[..., :diffs], axis=-1).reshape(-1, 2, diffs))
    sign = jnp.array([1.0, -1.0], jnp.float32)

    def meta_of(slab):
        got_pos = slab[0, 0, rows, : blocks * width].astype(jnp.int32).reshape(blocks, width)
        got_tg = slab[0, 0, rows + 1, : tg_flat.shape[0]].astype(jnp.int32).reshape(tile_group.shape)
        return one_hot(got_pos, True), got_tg

    perm1, tg1 = meta_of(got1[0])
    perm0, tg0 = meta_of(got0)
    lag10, relay_im = relay_lags(volts, perm, got1[0], got1[1], perm1, got0, perm0)
    perm2, tg2 = meta_of(relay_re)
    lag2 = pair_lags(mine[2][None].astype(jnp.int32), volts, perm, relay_re, relay_im, perm2, False)
    level_lags = {0: (lag10[1], tg0), 1: (lag10[0], tg1), 2: (lag2[0], tg2)}
    for bit in range(levels):
        lag, got_tg = level_lags[bit]
        lag = lag.reshape(2, 2, 2, 2 * width)[..., :diffs]
        fmask = (chan_ids == mine[bit]).astype(jnp.float32)
        w_direct = (tile_group[:, bit + 1, :, None] == group_ids).astype(jnp.float32)
        w_trans = jnp.swapaxes((got_tg[:, bit + 1, :, None] == group_ids).astype(jnp.float32), 0, 1)
        contrib_w.append(jnp.einsum("abg,f->abgf", w_direct, fmask).reshape(-1, groups_all, channels))
        contrib_v.append(jnp.flip(lag, axis=-1).reshape(-1, 2, diffs))
        contrib_w.append(jnp.einsum("abg,f->abgf", w_trans, fmask).reshape(-1, groups_all, channels))
        contrib_v.append((lag * sign[:, None]).reshape(-1, 2, diffs))
    dense = jnp.einsum(
        "ngf,nck->gfck", jnp.concatenate(contrib_w), jnp.concatenate(contrib_v), precision=HIGH
    )
    dense = dense * (1.0 / samples)
    dense = jnp.pad(dense, [(0, 0)] * 3 + [(0, 1)])
    dense = dense.reshape((n_inp, RG_DEV) + dense.shape[1:])
    return reduce_scatter(dense)[..., :diffs]


def solution(mesh):
    return jax.shard_map(
        on_device,
        mesh=mesh,
        in_specs=(P("freq", None, "inp", None), P("inp", None), P("inp", None, None)),
        out_specs=P("inp", "freq", None, None),
        check_vma=False,
    )
```

```python
import jax
import jax.numpy as jnp
from jax import lax
from jax.experimental import pallas as pl
from jax.experimental.pallas import tpu as pltpu
from jax.sharding import PartitionSpec as P

RG_DEV = 8
HIGH = lax.Precision.HIGHEST
NT = (((1,), (1,)), ((), ()))
MESH = pl.DeviceIdType.MESH


def lags_into(get_x, get_y, xperm_ref, yperm_ref, o_ref, slot, xs, ys):
    for blk in range(2):
        for c in range(2):
            xs[blk, c] = jnp.dot(xperm_ref[blk], get_x(blk, c), preferred_element_type=jnp.float32).astype(xs.dtype)
            ys[blk, c] = jnp.dot(yperm_ref[blk], get_y(blk, c), preferred_element_type=jnp.float32).astype(ys.dtype)
    dot = lambda u, v: lax.dot_general(u, v, NT, preferred_element_type=jnp.float32)
    for a in range(2):
        xre = xs[a, 0]
        xim = xs[a, 1]
        for b in range(2):
            yre = ys[b, 0]
            yim = ys[b, 1]
            real_part = dot(xre, yre) + dot(xim, yim)
            imag_part = dot(xim, yre) - dot(xre, yim)
            for c, part in enumerate((real_part, imag_part)):
                padded = jnp.concatenate([part, jnp.zeros_like(part)], axis=1)
                sheared = pltpu.roll(padded, 0, 1, stride=1, stride_axis=0)
                row = (a * 2 + b) * 2 + c
                o_ref[slot, pl.ds(row, 1), :] = jnp.sum(sheared, axis=0, keepdims=True)


def block_rows(ref, chan, c, blk, width):
    return ref[chan, c, pl.ds(blk * width, width), :]


def lag_kernel(sel_ref, xraw_ref, xperm_ref, y00, y01, y10, y11, yperm_ref, o_ref, xs, ys):
    width = xperm_ref.shape[1]
    ys_in = ((y00, y01), (y10, y11))
    lags_into(
        lambda a, c: block_rows(xraw_ref, 0, c, a, width),
        lambda b, c: ys_in[b][c][0, 0, pl.ds(0, width), :],
        xperm_ref, yperm_ref, o_ref, 0, xs, ys,
    )


def relay_kernel(x_ref, xperm_ref, y00, y01, y10, y11, yperm_ref, z_ref, zperm_ref,
                 o_ref, relay_ref, xs, ys, send_sem, recv_sem):
    width = xperm_ref.shape[1]
    me = lax.axis_index("inp")
    fq = lax.axis_index("freq")
    onward = lax.bitwise_xor(me, 6)
    barrier = pltpu.get_barrier_semaphore()
    pl.semaphore_signal(barrier, inc=1, device_id=(onward, fq), device_id_type=MESH)
    pl.semaphore_wait(barrier, 1)
    copy = pltpu.make_async_remote_copy(
        src_ref=y11,
        dst_ref=relay_ref,
        send_sem=send_sem,
        recv_sem=recv_sem,
        device_id=(onward, fq),
        device_id_type=MESH,
    )
    copy.start()
    parity = lax.bitwise_and(lax.bitwise_xor(lax.shift_right_logical(me, 1), lax.shift_right_logical(me, 2)), 1)
    ys_in = ((y00, y01), (y10, y11))
    lags_into(
        lambda a, c: block_rows(x_ref, parity, c, a, width),
        lambda b, c: ys_in[b][c][0, 0, pl.ds(0, width), :],
        xperm_ref, yperm_ref, o_ref, 0, xs, ys,
    )
    lags_into(
        lambda a, c: block_rows(x_ref, lax.bitwise_and(me, 1), c, a, width),
        lambda b, c: block_rows(z_ref, 0, c, b, width),
        xperm_ref, zperm_ref, o_ref, 1, xs, ys,
    )
    copy.wait()


def relay_lags(x_all, x_perm, y_parts, y_perm, z_all, z_perm):
    width = x_perm.shape[1]
    samples = x_all.shape[-1]
    vmem = pl.BlockSpec(memory_space=pltpu.VMEM)
    return pl.pallas_call(
        relay_kernel,
        out_shape=(
            jax.ShapeDtypeStruct((2, 8, 2 * width), jnp.float32),
            jax.ShapeDtypeStruct(y_parts[3].shape, y_parts[3].dtype),
        ),
        in_specs=[vmem] * 9,
        out_specs=(vmem, vmem),
        scratch_shapes=[
            pltpu.VMEM((2, 2, width, samples), x_all.dtype),
            pltpu.VMEM((2, 2, width, samples), x_all.dtype),
            pltpu.SemaphoreType.DMA(()),
            pltpu.SemaphoreType.DMA(()),
        ],
        compiler_params=pltpu.CompilerParams(
            collective_id=1, has_side_effects=True, vmem_limit_bytes=48 * 1024 * 1024
        ),
        cost_estimate=pl.CostEstimate(
            flops=2 * 4 * 24 * 2 * width * width * samples, transcendentals=0,
            bytes_accessed=4 * 2 * 4 * width * samples * 2,
        ),
    )(x_all, x_perm, *y_parts, y_perm, z_all, z_perm)


def pair_lags(sel, x_raw, x_perm, y_parts, y_perm, y_by_sel):
    n = sel.shape[0]
    _, _, rows_x, samples = x_raw.shape
    width = x_perm.shape[1]
    x_spec = pl.BlockSpec((1, 2, rows_x, samples), lambda i, s: (s[i], 0, 0, 0))
    if y_by_sel:
        y_specs = [
            pl.BlockSpec((1, 1, width, samples), lambda i, s, b=b, c=c: (s[i], c, b, 0))
            for b in range(2) for c in range(2)
        ]
        y_args = [y_parts] * 4
    else:
        y_specs = [
            pl.BlockSpec((1, 1) + part.shape[2:], lambda i, s: (0, 0, 0, 0)) for part in y_parts
        ]
        y_args = list(y_parts)
    perm_spec = pl.BlockSpec((2, width, width), lambda i, s: (0, 0, 0))
    out_spec = pl.BlockSpec((1, 8, 2 * width), lambda i, s: (i, 0, 0))
    flops = n * (16 + 8) * 2 * width * width * samples
    return pl.pallas_call(
        lag_kernel,
        out_shape=jax.ShapeDtypeStruct((n, 8, 2 * width), jnp.float32),
        grid_spec=pltpu.PrefetchScalarGridSpec(
            num_scalar_prefetch=1,
            grid=(n,),
            in_specs=[x_spec, perm_spec] + y_specs + [perm_spec],
            out_specs=out_spec,
            scratch_shapes=[
                pltpu.VMEM((2, 2, width, samples), x_raw.dtype),
                pltpu.VMEM((2, 2, width, samples), x_raw.dtype),
            ],
        ),
        compiler_params=pltpu.CompilerParams(vmem_limit_bytes=48 * 1024 * 1024),
        cost_estimate=pl.CostEstimate(
            flops=flops, transcendentals=0, bytes_accessed=n * 2 * 4 * width * samples * 2
        ),
    )(sel, x_raw, x_perm, *y_args, y_perm)


def scatter_kernel(dense_ref, out_ref, recv, send_sem, recv_sem):
    n = dense_ref.shape[0]
    me = lax.axis_index("inp")
    fq = lax.axis_index("freq")
    barrier = pltpu.get_barrier_semaphore()
    for o in range(1, n):
        pl.semaphore_signal(barrier, inc=1, device_id=(lax.rem(me + o, n), fq), device_id_type=MESH)
    pl.semaphore_wait(barrier, n - 1)
    copies = []
    for o in range(1, n):
        target = lax.rem(me + o, n)
        copy = pltpu.make_async_remote_copy(
            src_ref=dense_ref.at[target],
            dst_ref=recv.at[o - 1],
            send_sem=send_sem.at[o - 1],
            recv_sem=recv_sem.at[o - 1],
            device_id=(target, fq),
            device_id_type=MESH,
        )
        copy.start()
        copies.append(copy)
    for copy in copies:
        copy.wait()
    total = dense_ref[me]
    for o in range(n - 1):
        total = total + recv[o]
    out_ref[...] = total


def reduce_scatter(dense):
    n = dense.shape[0]
    slab = dense.shape[1:]
    return pl.pallas_call(
        scatter_kernel,
        out_shape=jax.ShapeDtypeStruct(slab, jnp.float32),
        in_specs=[pl.BlockSpec(memory_space=pltpu.VMEM)],
        out_specs=pl.BlockSpec(memory_space=pltpu.VMEM),
        scratch_shapes=[
            pltpu.VMEM((n - 1,) + slab, jnp.float32),
            pltpu.SemaphoreType.DMA((n - 1,)),
            pltpu.SemaphoreType.DMA((n - 1,)),
        ],
        compiler_params=pltpu.CompilerParams(collective_id=0, has_side_effects=True),
    )(dense)


def on_device(volts, position_input, tile_group):
    blocks, width = position_input.shape
    channels, _, rows, samples = volts.shape
    diffs = 2 * width - 1
    n_inp = lax.axis_size("inp")
    levels = n_inp.bit_length() - 1
    me = lax.axis_index("inp")

    pos_row = jnp.pad(position_input.reshape(-1), (0, samples - blocks * width))
    tg_flat = tile_group.reshape(-1)
    tg_row = jnp.pad(tg_flat, (0, samples - tg_flat.shape[0]))
    meta = jnp.stack([pos_row, tg_row]).astype(jnp.float32).astype(volts.dtype)
    meta = jnp.pad(meta[None], [(0, 1), (0, 14), (0, 0)])

    def chunks(chan):
        pick = lambda c, blk: jnp.where(chan == 1, volts[1, c, blk * width:(blk + 1) * width],
                                        volts[0, c, blk * width:(blk + 1) * width])
        parts = [pick(c, blk) for blk in range(2) for c in range(2)]
        parts[0] = jnp.concatenate([parts[0], meta[0]], axis=0)
        return [part[None, None] for part in parts]

    mine = [me & 1] + [((me >> 1) ^ (me >> 2)) & 1] * min(levels - 1, 2)
    mine += [(me >> bit) & 1 for bit in range(3, levels)]
    got1 = [lax.ppermute(part, "inp", [(i, i ^ 2) for i in range(n_inp)]) for part in chunks(1 - mine[1])]
    got0 = lax.ppermute(
        jnp.concatenate([jnp.where(mine[0] == 0, volts[1], volts[0]), meta], axis=1)[None],
        "inp",
        [(i, i ^ 1) for i in range(n_inp)],
    )
    relayed = [lax.ppermute(part, "inp", [(i, i ^ 6) for i in range(n_inp)]) for part in got1[:3]]

    ids = jnp.arange(width, dtype=jnp.int32)

    def one_hot(pos, reverse):
        if reverse:
            pos = pos[:, ::-1]
        return (pos[:, :, None] == ids[None, None, :]).astype(volts.dtype)

    perm = one_hot(position_input, False)
    perm_rev = one_hot(position_input, True)

    groups_all = RG_DEV * n_inp
    group_ids = jnp.arange(groups_all, dtype=jnp.int32)
    chan_ids = jnp.arange(channels, dtype=jnp.int32)

    lag0 = pair_lags(jnp.arange(channels, dtype=jnp.int32), volts, perm, volts, perm_rev, True)
    lag0 = lag0.reshape(channels, 2, 2, 2, 2 * width)
    center = (jnp.arange(2 * width) == width - 1)
    same = jnp.eye(2, dtype=bool)
    lag0 = jnp.where(same[None, :, :, None, None] & center[None, None, None, None, :], 0.0, lag0)
    contrib_w = []
    contrib_v = []
    w0 = (tile_group[:, 0, :, None] == group_ids).astype(jnp.float32)
    f0 = (chan_ids[:, None] == chan_ids[None, :]).astype(jnp.float32)
    contrib_w.append(jnp.einsum("abg,fh->fabgh", w0, f0).reshape(-1, groups_all, channels))
    contrib_v.append(jnp.flip(lag0[..., :diffs], axis=-1).reshape(-1, 2, diffs))
    sign = jnp.array([1.0, -1.0], jnp.float32)

    def meta_of(slab, row):
        got_pos = slab[0, 0, row, : blocks * width].astype(jnp.int32).reshape(blocks, width)
        got_tg = slab[0, 0, row + 1, : tg_flat.shape[0]].astype(jnp.int32).reshape(tile_group.shape)
        return one_hot(got_pos, True), got_tg

    perm1, tg1 = meta_of(got1[0], width)
    perm0, tg0 = meta_of(got0, rows)
    lag10, relay_last = relay_lags(volts, perm, got1, perm1, got0, perm0)
    perm2, tg2 = meta_of(relayed[0], width)
    lag2 = pair_lags(mine[2][None].astype(jnp.int32), volts, perm, relayed + [relay_last], perm2, False)
    level_lags = {0: (lag10[1], tg0), 1: (lag10[0], tg1), 2: (lag2[0], tg2)}
    for bit in range(levels):
        lag, got_tg = level_lags[bit]
        lag = lag.reshape(2, 2, 2, 2 * width)[..., :diffs]
        fmask = (chan_ids == mine[bit]).astype(jnp.float32)
        w_direct = (tile_group[:, bit + 1, :, None] == group_ids).astype(jnp.float32)
        w_trans = jnp.swapaxes((got_tg[:, bit + 1, :, None] == group_ids).astype(jnp.float32), 0, 1)
        contrib_w.append(jnp.einsum("abg,f->abgf", w_direct, fmask).reshape(-1, groups_all, channels))
        contrib_v.append(jnp.flip(lag, axis=-1).reshape(-1, 2, diffs))
        contrib_w.append(jnp.einsum("abg,f->abgf", w_trans, fmask).reshape(-1, groups_all, channels))
        contrib_v.append((lag * sign[:, None]).reshape(-1, 2, diffs))
    dense = jnp.einsum(
        "ngf,nck->gfck", jnp.concatenate(contrib_w), jnp.concatenate(contrib_v), precision=HIGH
    )
    dense = dense * (1.0 / samples)
    dense = jnp.pad(dense, [(0, 0)] * 3 + [(0, 1)])
    dense = dense.reshape((n_inp, RG_DEV) + dense.shape[1:])
    return reduce_scatter(dense)[..., :diffs]


def solution(mesh):
    return jax.shard_map(
        on_device,
        mesh=mesh,
        in_specs=(P("freq", None, "inp", None), P("inp", None), P("inp", None, None)),
        out_specs=P("inp", "freq", None, None),
        check_vma=False,
    )
```

```python
import jax
import jax.numpy as jnp
from jax import lax
from jax.experimental import pallas as pl
from jax.experimental.pallas import tpu as pltpu
from jax.sharding import PartitionSpec as P

RG_DEV = 8
HIGH = lax.Precision.HIGHEST
NT = (((1,), (1,)), ((), ()))
MESH = pl.DeviceIdType.MESH


def lags_into(get_x, get_y, xperm_ref, yperm_ref, o_ref, slot, xs, ys):
    for blk in range(2):
        for c in range(2):
            xs[blk, c] = jnp.dot(xperm_ref[blk], get_x(blk, c), preferred_element_type=jnp.float32).astype(xs.dtype)
            ys[blk, c] = jnp.dot(yperm_ref[blk], get_y(blk, c), preferred_element_type=jnp.float32).astype(ys.dtype)
    dot = lambda u, v: lax.dot_general(u, v, NT, preferred_element_type=jnp.float32)
    for a in range(2):
        xre = xs[a, 0]
        xim = xs[a, 1]
        for b in range(2):
            yre = ys[b, 0]
            yim = ys[b, 1]
            real_part = dot(xre, yre) + dot(xim, yim)
            imag_part = dot(xim, yre) - dot(xre, yim)
            for c, part in enumerate((real_part, imag_part)):
                padded = jnp.concatenate([part, jnp.zeros_like(part)], axis=1)
                sheared = pltpu.roll(padded, 0, 1, stride=1, stride_axis=0)
                row = (a * 2 + b) * 2 + c
                o_ref[slot, pl.ds(row, 1), :] = jnp.sum(sheared, axis=0, keepdims=True)


def block_rows(ref, chan, c, blk, width):
    return ref[chan, c, pl.ds(blk * width, width), :]


def lag_kernel(sel_ref, xraw_ref, xperm_ref, y00, y01, y10, y11, yperm_ref, o_ref, xs, ys):
    width = xperm_ref.shape[1]
    ys_in = ((y00, y01), (y10, y11))
    lags_into(
        lambda a, c: block_rows(xraw_ref, 0, c, a, width),
        lambda b, c: ys_in[b][c][0, 0, pl.ds(0, width), :],
        xperm_ref, yperm_ref, o_ref, 0, xs, ys,
    )


def start_relay(src_ref, dst_ref, send_sem, recv_sem):
    me = lax.axis_index("inp")
    fq = lax.axis_index("freq")
    onward = lax.bitwise_xor(me, 6)
    barrier = pltpu.get_barrier_semaphore()
    pl.semaphore_signal(barrier, inc=1, device_id=(onward, fq), device_id_type=MESH)
    pl.semaphore_wait(barrier, 1)
    copy = pltpu.make_async_remote_copy(
        src_ref=src_ref,
        dst_ref=dst_ref,
        send_sem=send_sem,
        recv_sem=recv_sem,
        device_id=(onward, fq),
        device_id_type=MESH,
    )
    copy.start()
    return copy


def relay_only_kernel(chunk_ref, prev_ref, relay_ref, send_sem, recv_sem):
    del prev_ref
    start_relay(chunk_ref, relay_ref, send_sem, recv_sem).wait()


def relay_own_kernel(chunk_ref, x_ref, xperm_ref, yperm_ref, o_ref, relay_ref, xs, ys, send_sem, recv_sem):
    width = xperm_ref.shape[1]
    copy = start_relay(chunk_ref, relay_ref, send_sem, recv_sem)
    for f in range(x_ref.shape[0]):
        lags_into(
            lambda a, c, f=f: block_rows(x_ref, f, c, a, width),
            lambda b, c, f=f: block_rows(x_ref, f, c, b, width),
            xperm_ref, yperm_ref, o_ref, f, xs, ys,
        )
    copy.wait()


def relay_kernel(x_ref, xperm_ref, y00, y01, y10, y11, yperm_ref, z_ref, zperm_ref, prev_ref,
                 o_ref, relay_ref, xs, ys, send_sem, recv_sem):
    del prev_ref
    width = xperm_ref.shape[1]
    me = lax.axis_index("inp")
    copy = start_relay(y11, relay_ref, send_sem, recv_sem)
    parity = lax.bitwise_and(lax.bitwise_xor(lax.shift_right_logical(me, 1), lax.shift_right_logical(me, 2)), 1)
    ys_in = ((y00, y01), (y10, y11))
    lags_into(
        lambda a, c: block_rows(x_ref, parity, c, a, width),
        lambda b, c: ys_in[b][c][0, 0, pl.ds(0, width), :],
        xperm_ref, yperm_ref, o_ref, 0, xs, ys,
    )
    lags_into(
        lambda a, c: block_rows(x_ref, lax.bitwise_and(me, 1), c, a, width),
        lambda b, c: block_rows(z_ref, 0, c, b, width),
        xperm_ref, zperm_ref, o_ref, 1, xs, ys,
    )
    copy.wait()


def relay_call(kernel, args, outs, n_lags, width, samples, collective_id):
    vmem = pl.BlockSpec(memory_space=pltpu.VMEM)
    scratch = []
    if n_lags:
        outs = (jax.ShapeDtypeStruct((n_lags, 8, 2 * width), jnp.float32),) + outs
        scratch = [pltpu.VMEM((2, 2, width, samples), jnp.bfloat16)] * 2
    return pl.pallas_call(
        kernel,
        out_shape=outs,
        in_specs=[vmem] * len(args),
        out_specs=tuple(vmem for _ in outs),
        scratch_shapes=scratch + [pltpu.SemaphoreType.DMA(()), pltpu.SemaphoreType.DMA(())],
        compiler_params=pltpu.CompilerParams(
            collective_id=collective_id, has_side_effects=True, vmem_limit_bytes=48 * 1024 * 1024
        ),
        cost_estimate=pl.CostEstimate(
            flops=max(n_lags, 1) * 4 * 24 * 2 * width * width * samples, transcendentals=0,
            bytes_accessed=4 * 2 * 4 * width * samples * 2,
        ),
    )(*args)


def pair_lags(sel, x_raw, x_perm, y_parts, y_perm, y_by_sel):
    n = sel.shape[0]
    _, _, rows_x, samples = x_raw.shape
    width = x_perm.shape[1]
    x_spec = pl.BlockSpec((1, 2, rows_x, samples), lambda i, s: (s[i], 0, 0, 0))
    if y_by_sel:
        y_specs = [
            pl.BlockSpec((1, 1, width, samples), lambda i, s, b=b, c=c: (s[i], c, b, 0))
            for b in range(2) for c in range(2)
        ]
        y_args = [y_parts] * 4
    else:
        y_specs = [
            pl.BlockSpec((1, 1) + part.shape[2:], lambda i, s: (0, 0, 0, 0)) for part in y_parts
        ]
        y_args = list(y_parts)
    perm_spec = pl.BlockSpec((2, width, width), lambda i, s: (0, 0, 0))
    out_spec = pl.BlockSpec((1, 8, 2 * width), lambda i, s: (i, 0, 0))
    flops = n * (16 + 8) * 2 * width * width * samples
    return pl.pallas_call(
        lag_kernel,
        out_shape=jax.ShapeDtypeStruct((n, 8, 2 * width), jnp.float32),
        grid_spec=pltpu.PrefetchScalarGridSpec(
            num_scalar_prefetch=1,
            grid=(n,),
            in_specs=[x_spec, perm_spec] + y_specs + [perm_spec],
            out_specs=out_spec,
            scratch_shapes=[
                pltpu.VMEM((2, 2, width, samples), x_raw.dtype),
                pltpu.VMEM((2, 2, width, samples), x_raw.dtype),
            ],
        ),
        compiler_params=pltpu.CompilerParams(vmem_limit_bytes=48 * 1024 * 1024),
        cost_estimate=pl.CostEstimate(
            flops=flops, transcendentals=0, bytes_accessed=n * 2 * 4 * width * samples * 2
        ),
    )(sel, x_raw, x_perm, *y_args, y_perm)


def scatter_kernel(dense_ref, out_ref, recv, send_sem, recv_sem):
    n = dense_ref.shape[0]
    me = lax.axis_index("inp")
    fq = lax.axis_index("freq")
    barrier = pltpu.get_barrier_semaphore()
    for o in range(1, n):
        pl.semaphore_signal(barrier, inc=1, device_id=(lax.rem(me + o, n), fq), device_id_type=MESH)
    pl.semaphore_wait(barrier, n - 1)
    copies = []
    for o in range(1, n):
        target = lax.rem(me + o, n)
        copy = pltpu.make_async_remote_copy(
            src_ref=dense_ref.at[target],
            dst_ref=recv.at[o - 1],
            send_sem=send_sem.at[o - 1],
            recv_sem=recv_sem.at[o - 1],
            device_id=(target, fq),
            device_id_type=MESH,
        )
        copy.start()
        copies.append(copy)
    for copy in copies:
        copy.wait()
    total = dense_ref[me]
    for o in range(n - 1):
        total = total + recv[o]
    out_ref[...] = total


def reduce_scatter(dense):
    n = dense.shape[0]
    slab = dense.shape[1:]
    return pl.pallas_call(
        scatter_kernel,
        out_shape=jax.ShapeDtypeStruct(slab, jnp.float32),
        in_specs=[pl.BlockSpec(memory_space=pltpu.VMEM)],
        out_specs=pl.BlockSpec(memory_space=pltpu.VMEM),
        scratch_shapes=[
            pltpu.VMEM((n - 1,) + slab, jnp.float32),
            pltpu.SemaphoreType.DMA((n - 1,)),
            pltpu.SemaphoreType.DMA((n - 1,)),
        ],
        compiler_params=pltpu.CompilerParams(collective_id=0, has_side_effects=True),
    )(dense)


def on_device(volts, position_input, tile_group):
    blocks, width = position_input.shape
    channels, _, rows, samples = volts.shape
    diffs = 2 * width - 1
    n_inp = lax.axis_size("inp")
    levels = n_inp.bit_length() - 1
    me = lax.axis_index("inp")

    pos_row = jnp.pad(position_input.reshape(-1), (0, samples - blocks * width))
    tg_flat = tile_group.reshape(-1)
    tg_row = jnp.pad(tg_flat, (0, samples - tg_flat.shape[0]))
    meta = jnp.stack([pos_row, tg_row]).astype(jnp.float32).astype(volts.dtype)
    meta = jnp.pad(meta[None], [(0, 1), (0, 14), (0, 0)])

    def chunks(chan):
        pick = lambda c, blk: jnp.where(chan == 1, volts[1, c, blk * width:(blk + 1) * width],
                                        volts[0, c, blk * width:(blk + 1) * width])
        parts = [pick(c, blk) for blk in range(2) for c in range(2)]
        parts[0] = jnp.concatenate([parts[0], meta[0]], axis=0)
        return [part[None, None] for part in parts]

    mine = [me & 1] + [((me >> 1) ^ (me >> 2)) & 1] * min(levels - 1, 2)
    mine += [(me >> bit) & 1 for bit in range(3, levels)]
    got1 = [lax.ppermute(part, "inp", [(i, i ^ 2) for i in range(n_inp)]) for part in chunks(1 - mine[1])]
    got0 = lax.ppermute(
        jnp.concatenate([jnp.where(mine[0] == 0, volts[1], volts[0]), meta], axis=1)[None],
        "inp",
        [(i, i ^ 1) for i in range(n_inp)],
    )
    ids = jnp.arange(width, dtype=jnp.int32)

    def one_hot(pos, reverse):
        if reverse:
            pos = pos[:, ::-1]
        return (pos[:, :, None] == ids[None, None, :]).astype(volts.dtype)

    perm = one_hot(position_input, False)
    perm_rev = one_hot(position_input, True)

    groups_all = RG_DEV * n_inp
    group_ids = jnp.arange(groups_all, dtype=jnp.int32)
    chan_ids = jnp.arange(channels, dtype=jnp.int32)

    chunk_shape = lambda k: (jax.ShapeDtypeStruct(got1[k].shape, got1[k].dtype),)
    lag0, relay0 = relay_call(
        relay_own_kernel, (got1[0], volts, perm, perm_rev), chunk_shape(0), channels, width, samples, 1
    )
    (relay1,) = relay_call(relay_only_kernel, (got1[1], relay0), chunk_shape(1), 0, width, samples, 2)
    (relay2,) = relay_call(relay_only_kernel, (got1[2], relay1), chunk_shape(2), 0, width, samples, 3)
    relayed = [relay0, relay1, relay2]
    lag0 = lag0.reshape(channels, 2, 2, 2, 2 * width)
    center = (jnp.arange(2 * width) == width - 1)
    same = jnp.eye(2, dtype=bool)
    lag0 = jnp.where(same[None, :, :, None, None] & center[None, None, None, None, :], 0.0, lag0)
    contrib_w = []
    contrib_v = []
    w0 = (tile_group[:, 0, :, None] == group_ids).astype(jnp.float32)
    f0 = (chan_ids[:, None] == chan_ids[None, :]).astype(jnp.float32)
    contrib_w.append(jnp.einsum("abg,fh->fabgh", w0, f0).reshape(-1, groups_all, channels))
    contrib_v.append(jnp.flip(lag0[..., :diffs], axis=-1).reshape(-1, 2, diffs))
    sign = jnp.array([1.0, -1.0], jnp.float32)

    def meta_of(slab, row):
        got_pos = slab[0, 0, row, : blocks * width].astype(jnp.int32).reshape(blocks, width)
        got_tg = slab[0, 0, row + 1, : tg_flat.shape[0]].astype(jnp.int32).reshape(tile_group.shape)
        return one_hot(got_pos, True), got_tg

    perm1, tg1 = meta_of(got1[0], width)
    perm0, tg0 = meta_of(got0, rows)
    lag10, relay_last = relay_call(
        relay_kernel, (volts, perm, *got1, perm1, got0, perm0, relay2), chunk_shape(3), 2, width, samples, 4
    )
    perm2, tg2 = meta_of(relayed[0], width)
    lag2 = pair_lags(mine[2][None].astype(jnp.int32), volts, perm, relayed + [relay_last], perm2, False)
    level_lags = {0: (lag10[1], tg0), 1: (lag10[0], tg1), 2: (lag2[0], tg2)}
    for bit in range(levels):
        lag, got_tg = level_lags[bit]
        lag = lag.reshape(2, 2, 2, 2 * width)[..., :diffs]
        fmask = (chan_ids == mine[bit]).astype(jnp.float32)
        w_direct = (tile_group[:, bit + 1, :, None] == group_ids).astype(jnp.float32)
        w_trans = jnp.swapaxes((got_tg[:, bit + 1, :, None] == group_ids).astype(jnp.float32), 0, 1)
        contrib_w.append(jnp.einsum("abg,f->abgf", w_direct, fmask).reshape(-1, groups_all, channels))
        contrib_v.append(jnp.flip(lag, axis=-1).reshape(-1, 2, diffs))
        contrib_w.append(jnp.einsum("abg,f->abgf", w_trans, fmask).reshape(-1, groups_all, channels))
        contrib_v.append((lag * sign[:, None]).reshape(-1, 2, diffs))
    dense = jnp.einsum(
        "ngf,nck->gfck", jnp.concatenate(contrib_w), jnp.concatenate(contrib_v), precision=HIGH
    )
    dense = dense * (1.0 / samples)
    dense = jnp.pad(dense, [(0, 0)] * 3 + [(0, 1)])
    dense = dense.reshape((n_inp, RG_DEV) + dense.shape[1:])
    return reduce_scatter(dense)[..., :diffs]


def solution(mesh):
    return jax.shard_map(
        on_device,
        mesh=mesh,
        in_specs=(P("freq", None, "inp", None), P("inp", None), P("inp", None, None)),
        out_specs=P("inp", "freq", None, None),
        check_vma=False,
    )
```

```python
import functools

import jax
import jax.numpy as jnp
from jax import lax
from jax.experimental import pallas as pl
from jax.experimental.pallas import tpu as pltpu
from jax.sharding import PartitionSpec as P

RG_DEV = 8
HIGH = lax.Precision.HIGHEST
NT = (((1,), (1,)), ((), ()))
MESH = pl.DeviceIdType.MESH


def lags_into(get_x, get_y, xperm_ref, yperm_ref, o_ref, slot, xs, ys, b_list=(0, 1)):
    for blk in range(2):
        for c in range(2):
            xs[blk, c] = jnp.dot(xperm_ref[blk], get_x(blk, c), preferred_element_type=jnp.float32).astype(xs.dtype)
            if blk in b_list:
                ys[blk, c] = jnp.dot(yperm_ref[blk], get_y(blk, c), preferred_element_type=jnp.float32).astype(ys.dtype)
    dot = lambda u, v: lax.dot_general(u, v, NT, preferred_element_type=jnp.float32)
    for a in range(2):
        xre = xs[a, 0]
        xim = xs[a, 1]
        for b_at, b in enumerate(b_list):
            yre = ys[b, 0]
            yim = ys[b, 1]
            real_part = dot(xre, yre) + dot(xim, yim)
            imag_part = dot(xim, yre) - dot(xre, yim)
            for c, part in enumerate((real_part, imag_part)):
                padded = jnp.concatenate([part, jnp.zeros_like(part)], axis=1)
                sheared = pltpu.roll(padded, 0, 1, stride=1, stride_axis=0)
                row = (a * len(b_list) + b_at) * 2 + c
                o_ref[slot, pl.ds(row, 1), :] = jnp.sum(sheared, axis=0, keepdims=True)


def block_rows(ref, chan, c, blk, width):
    return ref[chan, c, pl.ds(blk * width, width), :]


def lag_kernel(b_list, sel_ref, xraw_ref, xperm_ref, y00, y01, y10, y11, yperm_ref, o_ref, xs, ys):
    width = xperm_ref.shape[1]
    ys_in = ((y00, y01), (y10, y11))
    lags_into(
        lambda a, c: block_rows(xraw_ref, 0, c, a, width),
        lambda b, c: ys_in[b][c][0, 0, pl.ds(0, width), :],
        xperm_ref, yperm_ref, o_ref, 0, xs, ys, b_list,
    )


def start_relay(src_ref, dst_ref, send_sem, recv_sem):
    me = lax.axis_index("inp")
    fq = lax.axis_index("freq")
    onward = lax.bitwise_xor(me, 6)
    barrier = pltpu.get_barrier_semaphore()
    pl.semaphore_signal(barrier, inc=1, device_id=(onward, fq), device_id_type=MESH)
    pl.semaphore_wait(barrier, 1)
    copy = pltpu.make_async_remote_copy(
        src_ref=src_ref,
        dst_ref=dst_ref,
        send_sem=send_sem,
        recv_sem=recv_sem,
        device_id=(onward, fq),
        device_id_type=MESH,
    )
    copy.start()
    return copy


def relay_only_kernel(chunk_ref, prev_ref, relay_ref, send_sem, recv_sem):
    del prev_ref
    start_relay(chunk_ref, relay_ref, send_sem, recv_sem).wait()


def relay_own_kernel(chunk_ref, x_ref, xperm_ref, yperm_ref, o_ref, relay_ref, xs, ys, send_sem, recv_sem):
    width = xperm_ref.shape[1]
    copy = start_relay(chunk_ref, relay_ref, send_sem, recv_sem)
    for f in range(x_ref.shape[0]):
        lags_into(
            lambda a, c, f=f: block_rows(x_ref, f, c, a, width),
            lambda b, c, f=f: block_rows(x_ref, f, c, b, width),
            xperm_ref, yperm_ref, o_ref, f, xs, ys,
        )
    copy.wait()


def relay_mid_kernel(chunk_ref, prev_ref, x_ref, xperm_ref, y00, y01, yperm_ref, r00, r01, rperm_ref,
                     o_ref, relay_ref, xs, ys, send_sem, recv_sem):
    del prev_ref
    width = xperm_ref.shape[1]
    me = lax.axis_index("inp")
    copy = start_relay(chunk_ref, relay_ref, send_sem, recv_sem)
    parity = lax.bitwise_and(lax.bitwise_xor(lax.shift_right_logical(me, 1), lax.shift_right_logical(me, 2)), 1)
    for slot, parts in enumerate(((y00, y01), (r00, r01))):
        lags_into(
            lambda a, c: block_rows(x_ref, parity, c, a, width),
            lambda b, c, parts=parts: parts[c][0, 0, pl.ds(0, width), :],
            xperm_ref, (yperm_ref, rperm_ref)[slot], o_ref, slot, xs, ys, (0,),
        )
    copy.wait()


def relay_kernel(x_ref, xperm_ref, y10, y11, yperm_ref, z_ref, zperm_ref, prev_ref,
                 o_ref, p_ref, relay_ref, xs, ys, send_sem, recv_sem):
    del prev_ref
    width = xperm_ref.shape[1]
    me = lax.axis_index("inp")
    copy = start_relay(y11, relay_ref, send_sem, recv_sem)
    parity = lax.bitwise_and(lax.bitwise_xor(lax.shift_right_logical(me, 1), lax.shift_right_logical(me, 2)), 1)
    parts = (y10, y11)
    lags_into(
        lambda a, c: block_rows(x_ref, parity, c, a, width),
        lambda b, c: parts[c][0, 0, pl.ds(0, width), :],
        xperm_ref, yperm_ref, o_ref, 0, xs, ys, (1,),
    )
    lags_into(
        lambda a, c: block_rows(x_ref, lax.bitwise_and(me, 1), c, a, width),
        lambda b, c: block_rows(z_ref, 0, c, b, width),
        xperm_ref, zperm_ref, p_ref, 0, xs, ys,
    )
    copy.wait()


def relay_call(kernel, args, outs, lag_shapes, width, samples, collective_id):
    vmem = pl.BlockSpec(memory_space=pltpu.VMEM)
    scratch = []
    if lag_shapes:
        outs = tuple(jax.ShapeDtypeStruct(s + (2 * width,), jnp.float32) for s in lag_shapes) + outs
        scratch = [pltpu.VMEM((2, 2, width, samples), jnp.bfloat16)] * 2
    return pl.pallas_call(
        kernel,
        out_shape=outs,
        in_specs=[vmem] * len(args),
        out_specs=tuple(vmem for _ in outs),
        scratch_shapes=scratch + [pltpu.SemaphoreType.DMA(()), pltpu.SemaphoreType.DMA(())],
        compiler_params=pltpu.CompilerParams(
            collective_id=collective_id, has_side_effects=True, vmem_limit_bytes=48 * 1024 * 1024
        ),
        cost_estimate=pl.CostEstimate(
            flops=max(len(lag_shapes), 1) * 4 * 24 * 2 * width * width * samples, transcendentals=0,
            bytes_accessed=4 * 2 * 4 * width * samples * 2,
        ),
    )(*args)


def pair_lags(sel, x_raw, x_perm, y_parts, y_perm, y_by_sel, b_list=(0, 1)):
    n = sel.shape[0]
    _, _, rows_x, samples = x_raw.shape
    width = x_perm.shape[1]
    x_spec = pl.BlockSpec((1, 2, rows_x, samples), lambda i, s: (s[i], 0, 0, 0))
    if y_by_sel:
        y_specs = [
            pl.BlockSpec((1, 1, width, samples), lambda i, s, b=b, c=c: (s[i], c, b, 0))
            for b in range(2) for c in range(2)
        ]
        y_args = [y_parts] * 4
    else:
        y_specs = [
            pl.BlockSpec((1, 1) + part.shape[2:], lambda i, s: (0, 0, 0, 0)) for part in y_parts
        ]
        y_args = list(y_parts)
    perm_spec = pl.BlockSpec((2, width, width), lambda i, s: (0, 0, 0))
    n_rows = 4 * len(b_list)
    out_spec = pl.BlockSpec((1, n_rows, 2 * width), lambda i, s: (i, 0, 0))
    flops = n * (8 * len(b_list) + 8) * 2 * width * width * samples
    return pl.pallas_call(
        functools.partial(lag_kernel, b_list),
        out_shape=jax.ShapeDtypeStruct((n, n_rows, 2 * width), jnp.float32),
        grid_spec=pltpu.PrefetchScalarGridSpec(
            num_scalar_prefetch=1,
            grid=(n,),
            in_specs=[x_spec, perm_spec] + y_specs + [perm_spec],
            out_specs=out_spec,
            scratch_shapes=[
                pltpu.VMEM((2, 2, width, samples), x_raw.dtype),
                pltpu.VMEM((2, 2, width, samples), x_raw.dtype),
            ],
        ),
        compiler_params=pltpu.CompilerParams(vmem_limit_bytes=48 * 1024 * 1024),
        cost_estimate=pl.CostEstimate(
            flops=flops, transcendentals=0, bytes_accessed=n * 2 * 4 * width * samples * 2
        ),
    )(sel, x_raw, x_perm, *y_args, y_perm)


def scatter_kernel(dense_ref, out_ref, recv, send_sem, recv_sem):
    n = dense_ref.shape[0]
    me = lax.axis_index("inp")
    fq = lax.axis_index("freq")
    barrier = pltpu.get_barrier_semaphore()
    for o in range(1, n):
        pl.semaphore_signal(barrier, inc=1, device_id=(lax.rem(me + o, n), fq), device_id_type=MESH)
    pl.semaphore_wait(barrier, n - 1)
    copies = []
    for o in range(1, n):
        target = lax.rem(me + o, n)
        copy = pltpu.make_async_remote_copy(
            src_ref=dense_ref.at[target],
            dst_ref=recv.at[o - 1],
            send_sem=send_sem.at[o - 1],
            recv_sem=recv_sem.at[o - 1],
            device_id=(target, fq),
            device_id_type=MESH,
        )
        copy.start()
        copies.append(copy)
    for copy in copies:
        copy.wait()
    total = dense_ref[me]
    for o in range(n - 1):
        total = total + recv[o]
    out_ref[...] = total


def reduce_scatter(dense):
    n = dense.shape[0]
    slab = dense.shape[1:]
    return pl.pallas_call(
        scatter_kernel,
        out_shape=jax.ShapeDtypeStruct(slab, jnp.float32),
        in_specs=[pl.BlockSpec(memory_space=pltpu.VMEM)],
        out_specs=pl.BlockSpec(memory_space=pltpu.VMEM),
        scratch_shapes=[
            pltpu.VMEM((n - 1,) + slab, jnp.float32),
            pltpu.SemaphoreType.DMA((n - 1,)),
            pltpu.SemaphoreType.DMA((n - 1,)),
        ],
        compiler_params=pltpu.CompilerParams(collective_id=0, has_side_effects=True),
    )(dense)


def on_device(volts, position_input, tile_group):
    blocks, width = position_input.shape
    channels, _, rows, samples = volts.shape
    diffs = 2 * width - 1
    n_inp = lax.axis_size("inp")
    levels = n_inp.bit_length() - 1
    me = lax.axis_index("inp")

    pos_row = jnp.pad(position_input.reshape(-1), (0, samples - blocks * width))
    tg_flat = tile_group.reshape(-1)
    tg_row = jnp.pad(tg_flat, (0, samples - tg_flat.shape[0]))
    meta = jnp.stack([pos_row, tg_row]).astype(jnp.float32).astype(volts.dtype)
    meta = jnp.pad(meta[None], [(0, 1), (0, 14), (0, 0)])

    def chunks(chan):
        pick = lambda c, blk: jnp.where(chan == 1, volts[1, c, blk * width:(blk + 1) * width],
                                        volts[0, c, blk * width:(blk + 1) * width])
        parts = [pick(c, blk) for blk in range(2) for c in range(2)]
        parts[0] = jnp.concatenate([parts[0], meta[0]], axis=0)
        return [part[None, None] for part in parts]

    mine = [me & 1] + [((me >> 1) ^ (me >> 2)) & 1] * min(levels - 1, 2)
    mine += [(me >> bit) & 1 for bit in range(3, levels)]
    got1 = [lax.ppermute(part, "inp", [(i, i ^ 2) for i in range(n_inp)]) for part in chunks(1 - mine[1])]
    got0 = lax.ppermute(
        jnp.concatenate([jnp.where(mine[0] == 0, volts[1], volts[0]), meta], axis=1)[None],
        "inp",
        [(i, i ^ 1) for i in range(n_inp)],
    )
    ids = jnp.arange(width, dtype=jnp.int32)

    def one_hot(pos, reverse):
        if reverse:
            pos = pos[:, ::-1]
        return (pos[:, :, None] == ids[None, None, :]).astype(volts.dtype)

    perm = one_hot(position_input, False)
    perm_rev = one_hot(position_input, True)

    groups_all = RG_DEV * n_inp
    group_ids = jnp.arange(groups_all, dtype=jnp.int32)
    chan_ids = jnp.arange(channels, dtype=jnp.int32)

    chunk_shape = lambda k: (jax.ShapeDtypeStruct(got1[k].shape, got1[k].dtype),)
    lag0, relay0 = relay_call(
        relay_own_kernel, (got1[0], volts, perm, perm_rev), chunk_shape(0), [(channels, 8)], width, samples, 1
    )
    (relay1,) = relay_call(relay_only_kernel, (got1[1], relay0), chunk_shape(1), [], width, samples, 2)
    lag0 = lag0.reshape(channels, 2, 2, 2, 2 * width)
    center = (jnp.arange(2 * width) == width - 1)
    same = jnp.eye(2, dtype=bool)
    lag0 = jnp.where(same[None, :, :, None, None] & center[None, None, None, None, :], 0.0, lag0)
    contrib_w = []
    contrib_v = []
    w0 = (tile_group[:, 0, :, None] == group_ids).astype(jnp.float32)
    f0 = (chan_ids[:, None] == chan_ids[None, :]).astype(jnp.float32)
    contrib_w.append(jnp.einsum("abg,fh->fabgh", w0, f0).reshape(-1, groups_all, channels))
    contrib_v.append(jnp.flip(lag0[..., :diffs], axis=-1).reshape(-1, 2, diffs))
    sign = jnp.array([1.0, -1.0], jnp.float32)

    def meta_of(slab, row):
        got_pos = slab[0, 0, row, : blocks * width].astype(jnp.int32).reshape(blocks, width)
        got_tg = slab[0, 0, row + 1, : tg_flat.shape[0]].astype(jnp.int32).reshape(tile_group.shape)
        return one_hot(got_pos, True), got_tg

    perm1, tg1 = meta_of(got1[0], width)
    perm2, tg2 = meta_of(relay0, width)
    lag_b0, relay2 = relay_call(
        relay_mid_kernel, (got1[2], relay1, volts, perm, got1[0], got1[1], perm1, relay0, relay1, perm2),
        chunk_shape(2), [(2, 4)], width, samples, 3,
    )
    got0, _ = lax.optimization_barrier((got0, relay2))
    perm0, tg0 = meta_of(got0, rows)
    lag1_b1, lag_bit0, relay3 = relay_call(
        relay_kernel, (volts, perm, got1[2], got1[3], perm1, got0, perm0, relay2),
        chunk_shape(3), [(1, 4), (1, 8)], width, samples, 4,
    )
    lag2_b1 = pair_lags(
        mine[2][None].astype(jnp.int32), volts, perm, [relay0, relay1, relay2, relay3], perm2, False, (1,)
    )
    lag1 = jnp.stack([lag_b0[0].reshape(2, 2, -1), lag1_b1[0].reshape(2, 2, -1)], axis=1)
    lag2 = jnp.stack([lag_b0[1].reshape(2, 2, -1), lag2_b1[0].reshape(2, 2, -1)], axis=1)
    level_lags = {0: (lag_bit0[0], tg0), 1: (lag1, tg1), 2: (lag2, tg2)}
    for bit in range(levels):
        lag, got_tg = level_lags[bit]
        lag = lag.reshape(2, 2, 2, 2 * width)[..., :diffs]
        fmask = (chan_ids == mine[bit]).astype(jnp.float32)
        w_direct = (tile_group[:, bit + 1, :, None] == group_ids).astype(jnp.float32)
        w_trans = jnp.swapaxes((got_tg[:, bit + 1, :, None] == group_ids).astype(jnp.float32), 0, 1)
        contrib_w.append(jnp.einsum("abg,f->abgf", w_direct, fmask).reshape(-1, groups_all, channels))
        contrib_v.append(jnp.flip(lag, axis=-1).reshape(-1, 2, diffs))
        contrib_w.append(jnp.einsum("abg,f->abgf", w_trans, fmask).reshape(-1, groups_all, channels))
        contrib_v.append((lag * sign[:, None]).reshape(-1, 2, diffs))
    dense = jnp.einsum(
        "ngf,nck->gfck", jnp.concatenate(contrib_w), jnp.concatenate(contrib_v), precision=HIGH
    )
    dense = dense * (1.0 / samples)
    dense = jnp.pad(dense, [(0, 0)] * 3 + [(0, 1)])
    dense = dense.reshape((n_inp, RG_DEV) + dense.shape[1:])
    return reduce_scatter(dense)[..., :diffs]


def solution(mesh):
    return jax.shard_map(
        on_device,
        mesh=mesh,
        in_specs=(P("freq", None, "inp", None), P("inp", None), P("inp", None, None)),
        out_specs=P("inp", "freq", None, None),
        check_vma=False,
    )
```

```python
import functools

import jax
import jax.numpy as jnp
from jax import lax
from jax.experimental import pallas as pl
from jax.experimental.pallas import tpu as pltpu
from jax.sharding import PartitionSpec as P

RG_DEV = 8
HIGH = lax.Precision.HIGHEST
NT = (((1,), (1,)), ((), ()))
MESH = pl.DeviceIdType.MESH


def lags_into(get_x, get_y, xperm_ref, yperm_ref, o_ref, slot, xs, ys, b_list=(0, 1)):
    for blk in range(2):
        for c in range(2):
            xs[blk, c] = jnp.dot(xperm_ref[blk], get_x(blk, c), preferred_element_type=jnp.float32).astype(xs.dtype)
            if blk in b_list:
                ys[blk, c] = jnp.dot(yperm_ref[blk], get_y(blk, c), preferred_element_type=jnp.float32).astype(ys.dtype)
    dot = lambda u, v: lax.dot_general(u, v, NT, preferred_element_type=jnp.float32)
    for a in range(2):
        xre = xs[a, 0]
        xim = xs[a, 1]
        for b_at, b in enumerate(b_list):
            yre = ys[b, 0]
            yim = ys[b, 1]
            real_part = dot(xre, yre) + dot(xim, yim)
            imag_part = dot(xim, yre) - dot(xre, yim)
            for c, part in enumerate((real_part, imag_part)):
                padded = jnp.concatenate([part, jnp.zeros_like(part)], axis=1)
                sheared = pltpu.roll(padded, 0, 1, stride=1, stride_axis=0)
                row = (a * len(b_list) + b_at) * 2 + c
                o_ref[slot, pl.ds(row, 1), :] = jnp.sum(sheared, axis=0, keepdims=True)


def block_rows(ref, chan, c, blk, width):
    return ref[chan, c, pl.ds(blk * width, width), :]


def lag_kernel(b_list, sel_ref, xraw_ref, xperm_ref, y00, y01, y10, y11, yperm_ref, o_ref, xs, ys):
    width = xperm_ref.shape[1]
    ys_in = ((y00, y01), (y10, y11))
    lags_into(
        lambda a, c: block_rows(xraw_ref, 0, c, a, width),
        lambda b, c: ys_in[b][c][0, 0, pl.ds(0, width), :],
        xperm_ref, yperm_ref, o_ref, 0, xs, ys, b_list,
    )


def start_relay(src_ref, dst_ref, send_sem, recv_sem):
    me = lax.axis_index("inp")
    fq = lax.axis_index("freq")
    onward = lax.bitwise_xor(me, 6)
    barrier = pltpu.get_barrier_semaphore()
    pl.semaphore_signal(barrier, inc=1, device_id=(onward, fq), device_id_type=MESH)
    pl.semaphore_wait(barrier, 1)
    copy = pltpu.make_async_remote_copy(
        src_ref=src_ref,
        dst_ref=dst_ref,
        send_sem=send_sem,
        recv_sem=recv_sem,
        device_id=(onward, fq),
        device_id_type=MESH,
    )
    copy.start()
    return copy


def relay_only_kernel(chunk_ref, prev_ref, relay_ref, send_sem, recv_sem):
    del prev_ref
    start_relay(chunk_ref, relay_ref, send_sem, recv_sem).wait()


def relay_own_kernel(chunk_ref, x_ref, xperm_ref, yperm_ref, o_ref, relay_ref, xs, ys, send_sem, recv_sem):
    width = xperm_ref.shape[1]
    copy = start_relay(chunk_ref, relay_ref, send_sem, recv_sem)
    for f in range(x_ref.shape[0]):
        lags_into(
            lambda a, c, f=f: block_rows(x_ref, f, c, a, width),
            lambda b, c, f=f: block_rows(x_ref, f, c, b, width),
            xperm_ref, yperm_ref, o_ref, f, xs, ys,
        )
    copy.wait()


def relay_mid_kernel(chunk_ref, prev_ref, x_ref, xperm_ref, y00, y01, yperm_ref, r00, r01, rperm_ref,
                     o_ref, relay_ref, xs, ys, send_sem, recv_sem):
    del prev_ref
    width = xperm_ref.shape[1]
    me = lax.axis_index("inp")
    copy = start_relay(chunk_ref, relay_ref, send_sem, recv_sem)
    parity = lax.bitwise_and(lax.bitwise_xor(lax.shift_right_logical(me, 1), lax.shift_right_logical(me, 2)), 1)
    for slot, parts in enumerate(((y00, y01), (r00, r01))):
        lags_into(
            lambda a, c: block_rows(x_ref, parity, c, a, width),
            lambda b, c, parts=parts: parts[c][0, 0, pl.ds(0, width), :],
            xperm_ref, (yperm_ref, rperm_ref)[slot], o_ref, slot, xs, ys, (0,),
        )
    copy.wait()


def relay_kernel(x_ref, xperm_ref, y10, y11, yperm_ref, z_ref, zperm_ref, prev_ref,
                 o_ref, p_ref, relay_ref, xs, ys, send_sem, recv_sem):
    del prev_ref
    width = xperm_ref.shape[1]
    me = lax.axis_index("inp")
    copy = start_relay(y11, relay_ref, send_sem, recv_sem)
    parity = lax.bitwise_and(lax.bitwise_xor(lax.shift_right_logical(me, 1), lax.shift_right_logical(me, 2)), 1)
    parts = (y10, y11)
    lags_into(
        lambda a, c: block_rows(x_ref, parity, c, a, width),
        lambda b, c: parts[c][0, 0, pl.ds(0, width), :],
        xperm_ref, yperm_ref, o_ref, 0, xs, ys, (1,),
    )
    lags_into(
        lambda a, c: block_rows(x_ref, lax.bitwise_and(me, 1), c, a, width),
        lambda b, c: block_rows(z_ref, 0, c, b, width),
        xperm_ref, zperm_ref, p_ref, 0, xs, ys,
    )
    copy.wait()


def relay_call(kernel, args, outs, lag_shapes, width, samples, collective_id):
    vmem = pl.BlockSpec(memory_space=pltpu.VMEM)
    scratch = []
    if lag_shapes:
        outs = tuple(jax.ShapeDtypeStruct(s + (2 * width,), jnp.float32) for s in lag_shapes) + outs
        scratch = [pltpu.VMEM((2, 2, width, samples), jnp.bfloat16)] * 2
    return pl.pallas_call(
        kernel,
        out_shape=outs,
        in_specs=[vmem] * len(args),
        out_specs=tuple(vmem for _ in outs),
        scratch_shapes=scratch + [pltpu.SemaphoreType.DMA(()), pltpu.SemaphoreType.DMA(())],
        compiler_params=pltpu.CompilerParams(
            collective_id=collective_id, has_side_effects=True, vmem_limit_bytes=48 * 1024 * 1024
        ),
        cost_estimate=pl.CostEstimate(
            flops=max(len(lag_shapes), 1) * 4 * 24 * 2 * width * width * samples, transcendentals=0,
            bytes_accessed=4 * 2 * 4 * width * samples * 2,
        ),
    )(*args)


def pair_lags(sel, x_raw, x_perm, y_parts, y_perm, y_by_sel, b_list=(0, 1)):
    n = sel.shape[0]
    _, _, rows_x, samples = x_raw.shape
    width = x_perm.shape[1]
    x_spec = pl.BlockSpec((1, 2, rows_x, samples), lambda i, s: (s[i], 0, 0, 0))
    if y_by_sel:
        y_specs = [
            pl.BlockSpec((1, 1, width, samples), lambda i, s, b=b, c=c: (s[i], c, b, 0))
            for b in range(2) for c in range(2)
        ]
        y_args = [y_parts] * 4
    else:
        y_specs = [
            pl.BlockSpec((1, 1) + part.shape[2:], lambda i, s: (0, 0, 0, 0)) for part in y_parts
        ]
        y_args = list(y_parts)
    perm_spec = pl.BlockSpec((2, width, width), lambda i, s: (0, 0, 0))
    n_rows = 4 * len(b_list)
    out_spec = pl.BlockSpec((1, n_rows, 2 * width), lambda i, s: (i, 0, 0))
    flops = n * (8 * len(b_list) + 8) * 2 * width * width * samples
    return pl.pallas_call(
        functools.partial(lag_kernel, b_list),
        out_shape=jax.ShapeDtypeStruct((n, n_rows, 2 * width), jnp.float32),
        grid_spec=pltpu.PrefetchScalarGridSpec(
            num_scalar_prefetch=1,
            grid=(n,),
            in_specs=[x_spec, perm_spec] + y_specs + [perm_spec],
            out_specs=out_spec,
            scratch_shapes=[
                pltpu.VMEM((2, 2, width, samples), x_raw.dtype),
                pltpu.VMEM((2, 2, width, samples), x_raw.dtype),
            ],
        ),
        compiler_params=pltpu.CompilerParams(vmem_limit_bytes=48 * 1024 * 1024),
        cost_estimate=pl.CostEstimate(
            flops=flops, transcendentals=0, bytes_accessed=n * 2 * 4 * width * samples * 2
        ),
    )(sel, x_raw, x_perm, *y_args, y_perm)


def scatter_kernel(dense_ref, out_ref, recv, send_sem, recv_sem):
    n = dense_ref.shape[0]
    me = lax.axis_index("inp")
    fq = lax.axis_index("freq")
    barrier = pltpu.get_barrier_semaphore()
    for o in range(1, n):
        pl.semaphore_signal(barrier, inc=1, device_id=(lax.rem(me + o, n), fq), device_id_type=MESH)
    pl.semaphore_wait(barrier, n - 1)
    copies = []
    for o in range(1, n):
        target = lax.rem(me + o, n)
        copy = pltpu.make_async_remote_copy(
            src_ref=dense_ref.at[target],
            dst_ref=recv.at[o - 1],
            send_sem=send_sem.at[o - 1],
            recv_sem=recv_sem.at[o - 1],
            device_id=(target, fq),
            device_id_type=MESH,
        )
        copy.start()
        copies.append(copy)
    for copy in copies:
        copy.wait()
    total = dense_ref[me]
    for o in range(n - 1):
        total = total + recv[o]
    out_ref[...] = total


def reduce_scatter(dense):
    n = dense.shape[0]
    slab = dense.shape[1:]
    return pl.pallas_call(
        scatter_kernel,
        out_shape=jax.ShapeDtypeStruct(slab, jnp.float32),
        in_specs=[pl.BlockSpec(memory_space=pltpu.VMEM)],
        out_specs=pl.BlockSpec(memory_space=pltpu.VMEM),
        scratch_shapes=[
            pltpu.VMEM((n - 1,) + slab, jnp.float32),
            pltpu.SemaphoreType.DMA((n - 1,)),
            pltpu.SemaphoreType.DMA((n - 1,)),
        ],
        compiler_params=pltpu.CompilerParams(collective_id=0, has_side_effects=True),
    )(dense)


def on_device(volts, position_input, tile_group):
    blocks, width = position_input.shape
    channels, _, rows, samples = volts.shape
    diffs = 2 * width - 1
    n_inp = lax.axis_size("inp")
    levels = n_inp.bit_length() - 1
    me = lax.axis_index("inp")

    pos_row = jnp.pad(position_input.reshape(-1), (0, samples - blocks * width))
    tg_flat = tile_group.reshape(-1)
    tg_row = jnp.pad(tg_flat, (0, samples - tg_flat.shape[0]))
    meta = jnp.stack([pos_row, tg_row]).astype(jnp.float32).astype(volts.dtype)
    meta = jnp.pad(meta[None], [(0, 1), (0, 14), (0, 0)])

    def chunks(chan):
        pick = lambda c, blk: jnp.where(chan == 1, volts[1, c, blk * width:(blk + 1) * width],
                                        volts[0, c, blk * width:(blk + 1) * width])
        parts = [pick(c, blk) for blk in range(2) for c in range(2)]
        parts[0] = jnp.concatenate([parts[0], meta[0]], axis=0)
        return [part[None, None] for part in lax.optimization_barrier(tuple(parts))]

    mine = [me & 1] + [((me >> 1) ^ (me >> 2)) & 1] * min(levels - 1, 2)
    mine += [(me >> bit) & 1 for bit in range(3, levels)]
    got1 = [lax.ppermute(part, "inp", [(i, i ^ 2) for i in range(n_inp)]) for part in chunks(1 - mine[1])]
    got0 = lax.ppermute(
        jnp.concatenate([jnp.where(mine[0] == 0, volts[1], volts[0]), meta], axis=1)[None],
        "inp",
        [(i, i ^ 1) for i in range(n_inp)],
    )
    ids = jnp.arange(width, dtype=jnp.int32)

    def one_hot(pos, reverse):
        if reverse:
            pos = pos[:, ::-1]
        return (pos[:, :, None] == ids[None, None, :]).astype(volts.dtype)

    perm = one_hot(position_input, False)
    perm_rev = one_hot(position_input, True)

    groups_all = RG_DEV * n_inp
    group_ids = jnp.arange(groups_all, dtype=jnp.int32)
    chan_ids = jnp.arange(channels, dtype=jnp.int32)

    chunk_shape = lambda k: (jax.ShapeDtypeStruct(got1[k].shape, got1[k].dtype),)
    lag0, relay0 = relay_call(
        relay_own_kernel, (got1[0], volts, perm, perm_rev), chunk_shape(0), [(channels, 8)], width, samples, 1
    )
    (relay1,) = relay_call(relay_only_kernel, (got1[1], relay0), chunk_shape(1), [], width, samples, 2)
    lag0 = lag0.reshape(channels, 2, 2, 2, 2 * width)
    center = (jnp.arange(2 * width) == width - 1)
    same = jnp.eye(2, dtype=bool)
    lag0 = jnp.where(same[None, :, :, None, None] & center[None, None, None, None, :], 0.0, lag0)
    contrib_w = []
    contrib_v = []
    w0 = (tile_group[:, 0, :, None] == group_ids).astype(jnp.float32)
    f0 = (chan_ids[:, None] == chan_ids[None, :]).astype(jnp.float32)
    contrib_w.append(jnp.einsum("abg,fh->fabgh", w0, f0).reshape(-1, groups_all, channels))
    contrib_v.append(jnp.flip(lag0[..., :diffs], axis=-1).reshape(-1, 2, diffs))
    sign = jnp.array([1.0, -1.0], jnp.float32)

    def meta_of(slab, row):
        got_pos = slab[0, 0, row, : blocks * width].astype(jnp.int32).reshape(blocks, width)
        got_tg = slab[0, 0, row + 1, : tg_flat.shape[0]].astype(jnp.int32).reshape(tile_group.shape)
        return one_hot(got_pos, True), got_tg

    perm1, tg1 = meta_of(got1[0], width)
    perm2, tg2 = meta_of(relay0, width)
    lag_b0, relay2 = relay_call(
        relay_mid_kernel, (got1[2], relay1, volts, perm, got1[0], got1[1], perm1, relay0, relay1, perm2),
        chunk_shape(2), [(2, 4)], width, samples, 3,
    )
    got0, _ = lax.optimization_barrier((got0, relay2))
    perm0, tg0 = meta_of(got0, rows)
    lag1_b1, lag_bit0, relay3 = relay_call(
        relay_kernel, (volts, perm, got1[2], got1[3], perm1, got0, perm0, relay2),
        chunk_shape(3), [(1, 4), (1, 8)], width, samples, 4,
    )
    lag2_b1 = pair_lags(
        mine[2][None].astype(jnp.int32), volts, perm, [relay0, relay1, relay2, relay3], perm2, False, (1,)
    )
    lag1 = jnp.stack([lag_b0[0].reshape(2, 2, -1), lag1_b1[0].reshape(2, 2, -1)], axis=1)
    lag2 = jnp.stack([lag_b0[1].reshape(2, 2, -1), lag2_b1[0].reshape(2, 2, -1)], axis=1)
    level_lags = {0: (lag_bit0[0], tg0), 1: (lag1, tg1), 2: (lag2, tg2)}
    for bit in range(levels):
        lag, got_tg = level_lags[bit]
        lag = lag.reshape(2, 2, 2, 2 * width)[..., :diffs]
        fmask = (chan_ids == mine[bit]).astype(jnp.float32)
        w_direct = (tile_group[:, bit + 1, :, None] == group_ids).astype(jnp.float32)
        w_trans = jnp.swapaxes((got_tg[:, bit + 1, :, None] == group_ids).astype(jnp.float32), 0, 1)
        contrib_w.append(jnp.einsum("abg,f->abgf", w_direct, fmask).reshape(-1, groups_all, channels))
        contrib_v.append(jnp.flip(lag, axis=-1).reshape(-1, 2, diffs))
        contrib_w.append(jnp.einsum("abg,f->abgf", w_trans, fmask).reshape(-1, groups_all, channels))
        contrib_v.append((lag * sign[:, None]).reshape(-1, 2, diffs))
    dense = jnp.einsum(
        "ngf,nck->gfck", jnp.concatenate(contrib_w), jnp.concatenate(contrib_v), precision=HIGH
    )
    dense = dense * (1.0 / samples)
    dense = jnp.pad(dense, [(0, 0)] * 3 + [(0, 1)])
    dense = dense.reshape((n_inp, RG_DEV) + dense.shape[1:])
    return reduce_scatter(dense)[..., :diffs]


def solution(mesh):
    return jax.shard_map(
        on_device,
        mesh=mesh,
        in_specs=(P("freq", None, "inp", None), P("inp", None), P("inp", None, None)),
        out_specs=P("inp", "freq", None, None),
        check_vma=False,
    )
```

```python
import jax
import jax.numpy as jnp
from jax import lax
from jax.experimental import pallas as pl
from jax.experimental.pallas import tpu as pltpu
from jax.sharding import PartitionSpec as P

RG_DEV = 8
HIGH = lax.Precision.HIGHEST
NT = (((1,), (1,)), ((), ()))
MESH = pl.DeviceIdType.MESH


def lags_into(get_x, get_y, xperm_ref, yperm_ref, o_ref, slot, xs, ys):
    for blk in range(2):
        for c in range(2):
            xs[blk, c] = jnp.dot(xperm_ref[blk], get_x(blk, c), preferred_element_type=jnp.float32).astype(xs.dtype)
            ys[blk, c] = jnp.dot(yperm_ref[blk], get_y(blk, c), preferred_element_type=jnp.float32).astype(ys.dtype)
    dot = lambda u, v: lax.dot_general(u, v, NT, preferred_element_type=jnp.float32)
    for a in range(2):
        xre = xs[a, 0]
        xim = xs[a, 1]
        for b in range(2):
            yre = ys[b, 0]
            yim = ys[b, 1]
            real_part = dot(xre, yre) + dot(xim, yim)
            imag_part = dot(xim, yre) - dot(xre, yim)
            for c, part in enumerate((real_part, imag_part)):
                padded = jnp.concatenate([part, jnp.zeros_like(part)], axis=1)
                sheared = pltpu.roll(padded, 0, 1, stride=1, stride_axis=0)
                row = (a * 2 + b) * 2 + c
                o_ref[slot, pl.ds(row, 1), :] = jnp.sum(sheared, axis=0, keepdims=True)


def block_rows(ref, chan, c, blk, width):
    return ref[chan, c, pl.ds(blk * width, width), :]


def lag_kernel(sel_ref, xraw_ref, xperm_ref, y00, y01, y10, y11, yperm_ref, o_ref, xs, ys):
    width = xperm_ref.shape[1]
    ys_in = ((y00, y01), (y10, y11))
    lags_into(
        lambda a, c: block_rows(xraw_ref, 0, c, a, width),
        lambda b, c: ys_in[b][c][0, 0, pl.ds(0, width), :],
        xperm_ref, yperm_ref, o_ref, 0, xs, ys,
    )


def start_relay(src_ref, dst_ref, send_sem, recv_sem):
    me = lax.axis_index("inp")
    fq = lax.axis_index("freq")
    onward = lax.bitwise_xor(me, 6)
    barrier = pltpu.get_barrier_semaphore()
    pl.semaphore_signal(barrier, inc=1, device_id=(onward, fq), device_id_type=MESH)
    pl.semaphore_wait(barrier, 1)
    copy = pltpu.make_async_remote_copy(
        src_ref=src_ref,
        dst_ref=dst_ref,
        send_sem=send_sem,
        recv_sem=recv_sem,
        device_id=(onward, fq),
        device_id_type=MESH,
    )
    copy.start()
    return copy


def relay_only_kernel(chunk_ref, prev_ref, relay_ref, send_sem, recv_sem):
    del prev_ref
    start_relay(chunk_ref, relay_ref, send_sem, recv_sem).wait()


def relay_own_kernel(chunk_ref, x_ref, xperm_ref, yperm_ref, o_ref, relay_ref, xs, ys, send_sem, recv_sem):
    width = xperm_ref.shape[1]
    copy = start_relay(chunk_ref, relay_ref, send_sem, recv_sem)
    for f in range(x_ref.shape[0]):
        lags_into(
            lambda a, c, f=f: block_rows(x_ref, f, c, a, width),
            lambda b, c, f=f: block_rows(x_ref, f, c, b, width),
            xperm_ref, yperm_ref, o_ref, f, xs, ys,
        )
    copy.wait()


def relay_kernel(x_ref, xperm_ref, y00, y01, y10, y11, yperm_ref, z_ref, zperm_ref, prev_ref,
                 o_ref, relay_ref, xs, ys, send_sem, recv_sem):
    del prev_ref
    width = xperm_ref.shape[1]
    me = lax.axis_index("inp")
    copy = start_relay(y11, relay_ref, send_sem, recv_sem)
    parity = lax.bitwise_and(lax.bitwise_xor(lax.shift_right_logical(me, 1), lax.shift_right_logical(me, 2)), 1)
    ys_in = ((y00, y01), (y10, y11))
    lags_into(
        lambda a, c: block_rows(x_ref, parity, c, a, width),
        lambda b, c: ys_in[b][c][0, 0, pl.ds(0, width), :],
        xperm_ref, yperm_ref, o_ref, 0, xs, ys,
    )
    lags_into(
        lambda a, c: block_rows(x_ref, lax.bitwise_and(me, 1), c, a, width),
        lambda b, c: block_rows(z_ref, 0, c, b, width),
        xperm_ref, zperm_ref, o_ref, 1, xs, ys,
    )
    copy.wait()


def relay_call(kernel, args, outs, n_lags, width, samples, collective_id, hbm_args=()):
    vmem = pl.BlockSpec(memory_space=pltpu.VMEM)
    hbm = pl.BlockSpec(memory_space=pl.ANY)
    out_specs = tuple(hbm for _ in outs)
    scratch = []
    if n_lags:
        outs = (jax.ShapeDtypeStruct((n_lags, 8, 2 * width), jnp.float32),) + outs
        out_specs = (vmem,) + out_specs
        scratch = [pltpu.VMEM((2, 2, width, samples), jnp.bfloat16)] * 2
    return pl.pallas_call(
        kernel,
        out_shape=outs,
        in_specs=[hbm if i in hbm_args else vmem for i in range(len(args))],
        out_specs=out_specs,
        scratch_shapes=scratch + [pltpu.SemaphoreType.DMA(()), pltpu.SemaphoreType.DMA(())],
        compiler_params=pltpu.CompilerParams(
            collective_id=collective_id, has_side_effects=True, vmem_limit_bytes=48 * 1024 * 1024
        ),
        cost_estimate=pl.CostEstimate(
            flops=max(n_lags, 1) * 4 * 24 * 2 * width * width * samples, transcendentals=0,
            bytes_accessed=4 * 2 * 4 * width * samples * 2,
        ),
    )(*args)


def pair_lags(sel, x_raw, x_perm, y_parts, y_perm, y_by_sel):
    n = sel.shape[0]
    _, _, rows_x, samples = x_raw.shape
    width = x_perm.shape[1]
    x_spec = pl.BlockSpec((1, 2, rows_x, samples), lambda i, s: (s[i], 0, 0, 0))
    if y_by_sel:
        y_specs = [
            pl.BlockSpec((1, 1, width, samples), lambda i, s, b=b, c=c: (s[i], c, b, 0))
            for b in range(2) for c in range(2)
        ]
        y_args = [y_parts] * 4
    else:
        y_specs = [
            pl.BlockSpec((1, 1) + part.shape[2:], lambda i, s: (0, 0, 0, 0)) for part in y_parts
        ]
        y_args = list(y_parts)
    perm_spec = pl.BlockSpec((2, width, width), lambda i, s: (0, 0, 0))
    out_spec = pl.BlockSpec((1, 8, 2 * width), lambda i, s: (i, 0, 0))
    flops = n * (16 + 8) * 2 * width * width * samples
    return pl.pallas_call(
        lag_kernel,
        out_shape=jax.ShapeDtypeStruct((n, 8, 2 * width), jnp.float32),
        grid_spec=pltpu.PrefetchScalarGridSpec(
            num_scalar_prefetch=1,
            grid=(n,),
            in_specs=[x_spec, perm_spec] + y_specs + [perm_spec],
            out_specs=out_spec,
            scratch_shapes=[
                pltpu.VMEM((2, 2, width, samples), x_raw.dtype),
                pltpu.VMEM((2, 2, width, samples), x_raw.dtype),
            ],
        ),
        compiler_params=pltpu.CompilerParams(vmem_limit_bytes=48 * 1024 * 1024),
        cost_estimate=pl.CostEstimate(
            flops=flops, transcendentals=0, bytes_accessed=n * 2 * 4 * width * samples * 2
        ),
    )(sel, x_raw, x_perm, *y_args, y_perm)


def scatter_kernel(dense_ref, out_ref, recv, send_sem, recv_sem):
    n = dense_ref.shape[0]
    me = lax.axis_index("inp")
    fq = lax.axis_index("freq")
    barrier = pltpu.get_barrier_semaphore()
    for o in range(1, n):
        pl.semaphore_signal(barrier, inc=1, device_id=(lax.rem(me + o, n), fq), device_id_type=MESH)
    pl.semaphore_wait(barrier, n - 1)
    copies = []
    for o in range(1, n):
        target = lax.rem(me + o, n)
        copy = pltpu.make_async_remote_copy(
            src_ref=dense_ref.at[target],
            dst_ref=recv.at[o - 1],
            send_sem=send_sem.at[o - 1],
            recv_sem=recv_sem.at[o - 1],
            device_id=(target, fq),
            device_id_type=MESH,
        )
        copy.start()
        copies.append(copy)
    for copy in copies:
        copy.wait()
    total = dense_ref[me]
    for o in range(n - 1):
        total = total + recv[o]
    out_ref[...] = total


def reduce_scatter(dense):
    n = dense.shape[0]
    slab = dense.shape[1:]
    return pl.pallas_call(
        scatter_kernel,
        out_shape=jax.ShapeDtypeStruct(slab, jnp.float32),
        in_specs=[pl.BlockSpec(memory_space=pltpu.VMEM)],
        out_specs=pl.BlockSpec(memory_space=pltpu.VMEM),
        scratch_shapes=[
            pltpu.VMEM((n - 1,) + slab, jnp.float32),
            pltpu.SemaphoreType.DMA((n - 1,)),
            pltpu.SemaphoreType.DMA((n - 1,)),
        ],
        compiler_params=pltpu.CompilerParams(collective_id=0, has_side_effects=True),
    )(dense)


def on_device(volts, position_input, tile_group):
    blocks, width = position_input.shape
    channels, _, rows, samples = volts.shape
    diffs = 2 * width - 1
    n_inp = lax.axis_size("inp")
    levels = n_inp.bit_length() - 1
    me = lax.axis_index("inp")

    pos_row = jnp.pad(position_input.reshape(-1), (0, samples - blocks * width))
    tg_flat = tile_group.reshape(-1)
    tg_row = jnp.pad(tg_flat, (0, samples - tg_flat.shape[0]))
    meta = jnp.stack([pos_row, tg_row]).astype(jnp.float32).astype(volts.dtype)
    meta = jnp.pad(meta[None], [(0, 1), (0, 14), (0, 0)])

    def chunks(chan):
        pick = lambda c, blk: jnp.where(chan == 1, volts[1, c, blk * width:(blk + 1) * width],
                                        volts[0, c, blk * width:(blk + 1) * width])
        parts = [pick(c, blk) for blk in range(2) for c in range(2)]
        parts[0] = jnp.concatenate([parts[0], meta[0]], axis=0)
        return [part[None, None] for part in parts]

    mine = [me & 1] + [((me >> 1) ^ (me >> 2)) & 1] * min(levels - 1, 2)
    mine += [(me >> bit) & 1 for bit in range(3, levels)]
    got1 = [lax.ppermute(part, "inp", [(i, i ^ 2) for i in range(n_inp)]) for part in chunks(1 - mine[1])]
    got0 = lax.ppermute(
        jnp.concatenate([jnp.where(mine[0] == 0, volts[1], volts[0]), meta], axis=1)[None],
        "inp",
        [(i, i ^ 1) for i in range(n_inp)],
    )
    ids = jnp.arange(width, dtype=jnp.int32)

    def one_hot(pos, reverse):
        if reverse:
            pos = pos[:, ::-1]
        return (pos[:, :, None] == ids[None, None, :]).astype(volts.dtype)

    perm = one_hot(position_input, False)
    perm_rev = one_hot(position_input, True)

    groups_all = RG_DEV * n_inp
    group_ids = jnp.arange(groups_all, dtype=jnp.int32)
    chan_ids = jnp.arange(channels, dtype=jnp.int32)

    chunk_shape = lambda k: (jax.ShapeDtypeStruct(got1[k].shape, got1[k].dtype),)
    lag0, relay0 = relay_call(
        relay_own_kernel, (got1[0], volts, perm, perm_rev), chunk_shape(0), channels, width, samples, 1, (0,)
    )
    (relay1,) = relay_call(relay_only_kernel, (got1[1], relay0), chunk_shape(1), 0, width, samples, 2, (0, 1))
    (relay2,) = relay_call(relay_only_kernel, (got1[2], relay1), chunk_shape(2), 0, width, samples, 3, (0, 1))
    relayed = [relay0, relay1, relay2]
    lag0 = lag0.reshape(channels, 2, 2, 2, 2 * width)
    center = (jnp.arange(2 * width) == width - 1)
    same = jnp.eye(2, dtype=bool)
    lag0 = jnp.where(same[None, :, :, None, None] & center[None, None, None, None, :], 0.0, lag0)
    contrib_w = []
    contrib_v = []
    w0 = (tile_group[:, 0, :, None] == group_ids).astype(jnp.float32)
    f0 = (chan_ids[:, None] == chan_ids[None, :]).astype(jnp.float32)
    contrib_w.append(jnp.einsum("abg,fh->fabgh", w0, f0).reshape(-1, groups_all, channels))
    contrib_v.append(jnp.flip(lag0[..., :diffs], axis=-1).reshape(-1, 2, diffs))
    sign = jnp.array([1.0, -1.0], jnp.float32)

    def meta_of(slab, row):
        got_pos = slab[0, 0, row, : blocks * width].astype(jnp.int32).reshape(blocks, width)
        got_tg = slab[0, 0, row + 1, : tg_flat.shape[0]].astype(jnp.int32).reshape(tile_group.shape)
        return one_hot(got_pos, True), got_tg

    perm1, tg1 = meta_of(got1[0], width)
    perm0, tg0 = meta_of(got0, rows)
    lag10, relay_last = relay_call(
        relay_kernel, (volts, perm, *got1, perm1, got0, perm0, relay2), chunk_shape(3), 2, width, samples, 4, (9,)
    )
    perm2, tg2 = meta_of(relayed[0], width)
    lag2 = pair_lags(mine[2][None].astype(jnp.int32), volts, perm, relayed + [relay_last], perm2, False)
    level_lags = {0: (lag10[1], tg0), 1: (lag10[0], tg1), 2: (lag2[0], tg2)}
    for bit in range(levels):
        lag, got_tg = level_lags[bit]
        lag = lag.reshape(2, 2, 2, 2 * width)[..., :diffs]
        fmask = (chan_ids == mine[bit]).astype(jnp.float32)
        w_direct = (tile_group[:, bit + 1, :, None] == group_ids).astype(jnp.float32)
        w_trans = jnp.swapaxes((got_tg[:, bit + 1, :, None] == group_ids).astype(jnp.float32), 0, 1)
        contrib_w.append(jnp.einsum("abg,f->abgf", w_direct, fmask).reshape(-1, groups_all, channels))
        contrib_v.append(jnp.flip(lag, axis=-1).reshape(-1, 2, diffs))
        contrib_w.append(jnp.einsum("abg,f->abgf", w_trans, fmask).reshape(-1, groups_all, channels))
        contrib_v.append((lag * sign[:, None]).reshape(-1, 2, diffs))
    dense = jnp.einsum(
        "ngf,nck->gfck", jnp.concatenate(contrib_w), jnp.concatenate(contrib_v), precision=HIGH
    )
    dense = dense * (1.0 / samples)
    dense = jnp.pad(dense, [(0, 0)] * 3 + [(0, 1)])
    dense = dense.reshape((n_inp, RG_DEV) + dense.shape[1:])
    return reduce_scatter(dense)[..., :diffs]


def solution(mesh):
    return jax.shard_map(
        on_device,
        mesh=mesh,
        in_specs=(P("freq", None, "inp", None), P("inp", None), P("inp", None, None)),
        out_specs=P("inp", "freq", None, None),
        check_vma=False,
    )
```

```python
import jax
import jax.numpy as jnp
from jax import lax
from jax.experimental import pallas as pl
from jax.experimental.pallas import tpu as pltpu
from jax.sharding import PartitionSpec as P

RG_DEV = 8
HIGH = lax.Precision.HIGHEST
NT = (((1,), (1,)), ((), ()))
MESH = pl.DeviceIdType.MESH


def lags_into(get_x, get_y, xperm_ref, yperm_ref, o_ref, slot, xs, ys):
    for blk in range(2):
        for c in range(2):
            xs[blk, c] = jnp.dot(xperm_ref[blk], get_x(blk, c), preferred_element_type=jnp.float32).astype(xs.dtype)
            ys[blk, c] = jnp.dot(yperm_ref[blk], get_y(blk, c), preferred_element_type=jnp.float32).astype(ys.dtype)
    dot = lambda u, v: lax.dot_general(u, v, NT, preferred_element_type=jnp.float32)
    for a in range(2):
        xre = xs[a, 0]
        xim = xs[a, 1]
        for b in range(2):
            yre = ys[b, 0]
            yim = ys[b, 1]
            real_part = dot(xre, yre) + dot(xim, yim)
            imag_part = dot(xim, yre) - dot(xre, yim)
            for c, part in enumerate((real_part, imag_part)):
                padded = jnp.concatenate([part, jnp.zeros_like(part)], axis=1)
                sheared = pltpu.roll(padded, 0, 1, stride=1, stride_axis=0)
                row = (a * 2 + b) * 2 + c
                o_ref[slot, pl.ds(row, 1), :] = jnp.sum(sheared, axis=0, keepdims=True)


def block_rows(ref, chan, c, blk, width):
    return ref[chan, c, pl.ds(blk * width, width), :]


def lag_kernel(sel_ref, xraw_ref, xperm_ref, y00, y01, y10, y11, yperm_ref, o_ref, xs, ys):
    width = xperm_ref.shape[1]
    ys_in = ((y00, y01), (y10, y11))
    lags_into(
        lambda a, c: block_rows(xraw_ref, 0, c, a, width),
        lambda b, c: ys_in[b][c][0, 0, pl.ds(0, width), :],
        xperm_ref, yperm_ref, o_ref, 0, xs, ys,
    )


def start_relay(src_ref, dst_ref, send_sem, recv_sem):
    me = lax.axis_index("inp")
    fq = lax.axis_index("freq")
    onward = lax.bitwise_xor(me, 6)
    barrier = pltpu.get_barrier_semaphore()
    pl.semaphore_signal(barrier, inc=1, device_id=(onward, fq), device_id_type=MESH)
    pl.semaphore_wait(barrier, 1)
    copy = pltpu.make_async_remote_copy(
        src_ref=src_ref,
        dst_ref=dst_ref,
        send_sem=send_sem,
        recv_sem=recv_sem,
        device_id=(onward, fq),
        device_id_type=MESH,
    )
    copy.start()
    return copy


def relay_only_kernel(chunk_ref, prev_ref, relay_ref, send_sem, recv_sem):
    del prev_ref
    start_relay(chunk_ref, relay_ref, send_sem, recv_sem).wait()


def relay_own_kernel(chunk_ref, x_ref, xperm_ref, yperm_ref, o_ref, relay_ref, xs, ys, send_sem, recv_sem):
    width = xperm_ref.shape[1]
    copy = start_relay(chunk_ref, relay_ref, send_sem, recv_sem)
    for f in range(x_ref.shape[0]):
        lags_into(
            lambda a, c, f=f: block_rows(x_ref, f, c, a, width),
            lambda b, c, f=f: block_rows(x_ref, f, c, b, width),
            xperm_ref, yperm_ref, o_ref, f, xs, ys,
        )
    copy.wait()


def relay_kernel(x_ref, xperm_ref, y00, y01, y10, y11, yperm_ref, z_ref, zperm_ref, prev_ref,
                 o_ref, relay_ref, xs, ys, send_sem, recv_sem):
    del prev_ref
    width = xperm_ref.shape[1]
    me = lax.axis_index("inp")
    copy = start_relay(y11, relay_ref, send_sem, recv_sem)
    parity = lax.bitwise_and(lax.bitwise_xor(lax.shift_right_logical(me, 1), lax.shift_right_logical(me, 2)), 1)
    ys_in = ((y00, y01), (y10, y11))
    lags_into(
        lambda a, c: block_rows(x_ref, parity, c, a, width),
        lambda b, c: ys_in[b][c][0, 0, pl.ds(0, width), :],
        xperm_ref, yperm_ref, o_ref, 0, xs, ys,
    )
    lags_into(
        lambda a, c: block_rows(x_ref, lax.bitwise_and(me, 1), c, a, width),
        lambda b, c: block_rows(z_ref, 0, c, b, width),
        xperm_ref, zperm_ref, o_ref, 1, xs, ys,
    )
    copy.wait()


def relay_call(kernel, args, outs, n_lags, width, samples, collective_id, hbm_args=()):
    vmem = pl.BlockSpec(memory_space=pltpu.VMEM)
    hbm = pl.BlockSpec(memory_space=pl.ANY)
    out_specs = tuple(hbm for _ in outs)
    scratch = []
    if n_lags:
        outs = (jax.ShapeDtypeStruct((n_lags, 8, 2 * width), jnp.float32),) + outs
        out_specs = (vmem,) + out_specs
        scratch = [pltpu.VMEM((2, 2, width, samples), jnp.bfloat16)] * 2
    return pl.pallas_call(
        kernel,
        out_shape=outs,
        in_specs=[hbm if i in hbm_args else vmem for i in range(len(args))],
        out_specs=out_specs,
        scratch_shapes=scratch + [pltpu.SemaphoreType.DMA(()), pltpu.SemaphoreType.DMA(())],
        compiler_params=pltpu.CompilerParams(
            collective_id=collective_id, has_side_effects=True, vmem_limit_bytes=48 * 1024 * 1024
        ),
        cost_estimate=pl.CostEstimate(
            flops=max(n_lags, 1) * 4 * 24 * 2 * width * width * samples, transcendentals=0,
            bytes_accessed=4 * 2 * 4 * width * samples * 2,
        ),
    )(*args)


def pair_lags(sel, x_raw, x_perm, y_parts, y_perm, y_by_sel):
    n = sel.shape[0]
    _, _, rows_x, samples = x_raw.shape
    width = x_perm.shape[1]
    x_spec = pl.BlockSpec((1, 2, rows_x, samples), lambda i, s: (s[i], 0, 0, 0))
    if y_by_sel:
        y_specs = [
            pl.BlockSpec((1, 1, width, samples), lambda i, s, b=b, c=c: (s[i], c, b, 0))
            for b in range(2) for c in range(2)
        ]
        y_args = [y_parts] * 4
    else:
        y_specs = [
            pl.BlockSpec((1, 1) + part.shape[2:], lambda i, s: (0, 0, 0, 0)) for part in y_parts
        ]
        y_args = list(y_parts)
    perm_spec = pl.BlockSpec((2, width, width), lambda i, s: (0, 0, 0))
    out_spec = pl.BlockSpec((1, 8, 2 * width), lambda i, s: (i, 0, 0))
    flops = n * (16 + 8) * 2 * width * width * samples
    return pl.pallas_call(
        lag_kernel,
        out_shape=jax.ShapeDtypeStruct((n, 8, 2 * width), jnp.float32),
        grid_spec=pltpu.PrefetchScalarGridSpec(
            num_scalar_prefetch=1,
            grid=(n,),
            in_specs=[x_spec, perm_spec] + y_specs + [perm_spec],
            out_specs=out_spec,
            scratch_shapes=[
                pltpu.VMEM((2, 2, width, samples), x_raw.dtype),
                pltpu.VMEM((2, 2, width, samples), x_raw.dtype),
            ],
        ),
        compiler_params=pltpu.CompilerParams(vmem_limit_bytes=48 * 1024 * 1024),
        cost_estimate=pl.CostEstimate(
            flops=flops, transcendentals=0, bytes_accessed=n * 2 * 4 * width * samples * 2
        ),
    )(sel, x_raw, x_perm, *y_args, y_perm)


def scatter_kernel(dense_ref, out_ref, recv, send_sem, recv_sem):
    n = dense_ref.shape[0]
    me = lax.axis_index("inp")
    fq = lax.axis_index("freq")
    barrier = pltpu.get_barrier_semaphore()
    for o in range(1, n):
        pl.semaphore_signal(barrier, inc=1, device_id=(lax.rem(me + o, n), fq), device_id_type=MESH)
    pl.semaphore_wait(barrier, n - 1)
    copies = []
    for o in range(1, n):
        target = lax.rem(me + o, n)
        copy = pltpu.make_async_remote_copy(
            src_ref=dense_ref.at[target],
            dst_ref=recv.at[o - 1],
            send_sem=send_sem.at[o - 1],
            recv_sem=recv_sem.at[o - 1],
            device_id=(target, fq),
            device_id_type=MESH,
        )
        copy.start()
        copies.append(copy)
    for copy in copies:
        copy.wait()
    total = dense_ref[me]
    for o in range(n - 1):
        total = total + recv[o]
    out_ref[...] = total


def reduce_scatter(dense):
    n = dense.shape[0]
    slab = dense.shape[1:]
    return pl.pallas_call(
        scatter_kernel,
        out_shape=jax.ShapeDtypeStruct(slab, jnp.float32),
        in_specs=[pl.BlockSpec(memory_space=pltpu.VMEM)],
        out_specs=pl.BlockSpec(memory_space=pltpu.VMEM),
        scratch_shapes=[
            pltpu.VMEM((n - 1,) + slab, jnp.float32),
            pltpu.SemaphoreType.DMA((n - 1,)),
            pltpu.SemaphoreType.DMA((n - 1,)),
        ],
        compiler_params=pltpu.CompilerParams(collective_id=0, has_side_effects=True),
    )(dense)


def on_device(volts, position_input, tile_group):
    blocks, width = position_input.shape
    channels, _, rows, samples = volts.shape
    diffs = 2 * width - 1
    n_inp = lax.axis_size("inp")
    levels = n_inp.bit_length() - 1
    me = lax.axis_index("inp")

    pos_row = jnp.pad(position_input.reshape(-1), (0, samples - blocks * width))
    tg_flat = tile_group.reshape(-1)
    tg_row = jnp.pad(tg_flat, (0, samples - tg_flat.shape[0]))
    meta = jnp.stack([pos_row, tg_row]).astype(jnp.float32).astype(volts.dtype)
    meta = jnp.pad(meta[None], [(0, 1), (0, 14), (0, 0)])

    def chunks(chan):
        pick = lambda c, blk: jnp.where(chan == 1, volts[1, c, blk * width:(blk + 1) * width],
                                        volts[0, c, blk * width:(blk + 1) * width])
        parts = [pick(c, blk) for blk in range(2) for c in range(2)]
        parts[0] = jnp.concatenate([parts[0], meta[0]], axis=0)
        return [part[None, None] for part in parts]

    mine = [me & 1] + [((me >> 1) ^ (me >> 2)) & 1] * min(levels - 1, 2)
    mine += [(me >> bit) & 1 for bit in range(3, levels)]
    got1 = [lax.ppermute(part, "inp", [(i, i ^ 2) for i in range(n_inp)]) for part in chunks(1 - mine[1])]
    got0 = lax.ppermute(
        jnp.concatenate([jnp.where(mine[0] == 0, volts[1], volts[0]), meta], axis=1)[None],
        "inp",
        [(i, i ^ 1) for i in range(n_inp)],
    )
    ids = jnp.arange(width, dtype=jnp.int32)

    def one_hot(pos, reverse):
        if reverse:
            pos = pos[:, ::-1]
        return (pos[:, :, None] == ids[None, None, :]).astype(volts.dtype)

    perm = one_hot(position_input, False)
    perm_rev = one_hot(position_input, True)

    groups_all = RG_DEV * n_inp
    group_ids = jnp.arange(groups_all, dtype=jnp.int32)
    chan_ids = jnp.arange(channels, dtype=jnp.int32)

    chunk_shape = lambda k: (jax.ShapeDtypeStruct(got1[k].shape, got1[k].dtype),)
    lag0, relay0 = relay_call(
        relay_own_kernel, (got1[0], volts, perm, perm_rev), chunk_shape(0), channels, width, samples, 1, (0,)
    )
    (relay1,) = relay_call(relay_only_kernel, (got1[1], relay0), chunk_shape(1), 0, width, samples, 2, (0, 1))
    (relay2,) = relay_call(relay_only_kernel, (got1[2], relay1), chunk_shape(2), 0, width, samples, 3, (0, 1))
    relayed = [relay0, relay1, relay2]
    lag0 = lag0.reshape(channels, 2, 2, 2, 2 * width)
    center = (jnp.arange(2 * width) == width - 1)
    same = jnp.eye(2, dtype=bool)
    lag0 = jnp.where(same[None, :, :, None, None] & center[None, None, None, None, :], 0.0, lag0)
    def flip_lags(lag):
        return jnp.concatenate([jnp.flip(lag[..., :diffs], axis=-1), jnp.zeros_like(lag[..., diffs:])], axis=-1)

    contrib_w = []
    contrib_v = []
    w0 = (tile_group[:, 0, :, None] == group_ids).astype(jnp.float32)
    f0 = (chan_ids[:, None] == chan_ids[None, :]).astype(jnp.float32)
    contrib_w.append(jnp.einsum("abg,fh->fabgh", w0, f0).reshape(-1, groups_all, channels))
    contrib_v.append(flip_lags(lag0).reshape(-1, 2, 2 * width))
    sign = jnp.array([1.0, -1.0], jnp.float32)

    def meta_of(slab, row):
        got_pos = slab[0, 0, row, : blocks * width].astype(jnp.int32).reshape(blocks, width)
        got_tg = slab[0, 0, row + 1, : tg_flat.shape[0]].astype(jnp.int32).reshape(tile_group.shape)
        return one_hot(got_pos, True), got_tg

    perm1, tg1 = meta_of(got1[0], width)
    perm0, tg0 = meta_of(got0, rows)
    lag10, relay_last = relay_call(
        relay_kernel, (volts, perm, *got1, perm1, got0, perm0, relay2), chunk_shape(3), 2, width, samples, 4, (9,)
    )
    perm2, tg2 = meta_of(relayed[0], width)
    lag2 = pair_lags(mine[2][None].astype(jnp.int32), volts, perm, relayed + [relay_last], perm2, False)
    level_lags = {0: (lag10[1], tg0), 1: (lag10[0], tg1), 2: (lag2[0], tg2)}
    for bit in range(levels):
        lag, got_tg = level_lags[bit]
        lag = lag.reshape(2, 2, 2, 2 * width)
        fmask = (chan_ids == mine[bit]).astype(jnp.float32)
        w_direct = (tile_group[:, bit + 1, :, None] == group_ids).astype(jnp.float32)
        w_trans = jnp.swapaxes((got_tg[:, bit + 1, :, None] == group_ids).astype(jnp.float32), 0, 1)
        contrib_w.append(jnp.einsum("abg,f->abgf", w_direct, fmask).reshape(-1, groups_all, channels))
        contrib_v.append(flip_lags(lag).reshape(-1, 2, 2 * width))
        contrib_w.append(jnp.einsum("abg,f->abgf", w_trans, fmask).reshape(-1, groups_all, channels))
        contrib_v.append((lag * sign[:, None]).reshape(-1, 2, 2 * width))
    dense = jnp.einsum(
        "ngf,nck->gfck", jnp.concatenate(contrib_w), jnp.concatenate(contrib_v), precision=HIGH
    )
    dense = dense * (1.0 / samples)
    dense = dense.reshape((n_inp, RG_DEV) + dense.shape[1:])
    return reduce_scatter(dense)[..., :diffs]


def solution(mesh):
    return jax.shard_map(
        on_device,
        mesh=mesh,
        in_specs=(P("freq", None, "inp", None), P("inp", None), P("inp", None, None)),
        out_specs=P("inp", "freq", None, None),
        check_vma=False,
    )
```

```python
import jax
import jax.numpy as jnp
from jax import lax
from jax.experimental import pallas as pl
from jax.experimental.pallas import tpu as pltpu
from jax.sharding import PartitionSpec as P

RG_DEV = 8
HIGH = lax.Precision.HIGHEST
NT = (((1,), (1,)), ((), ()))
MESH = pl.DeviceIdType.MESH


def lags_into(get_x, get_y, xperm_ref, yperm_ref, o_ref, slot, xs, ys):
    for blk in range(2):
        for c in range(2):
            xs[blk, c] = jnp.dot(xperm_ref[blk], get_x(blk, c), preferred_element_type=jnp.float32).astype(xs.dtype)
            ys[blk, c] = jnp.dot(yperm_ref[blk], get_y(blk, c), preferred_element_type=jnp.float32).astype(ys.dtype)
    dot = lambda u, v: lax.dot_general(u, v, NT, preferred_element_type=jnp.float32)
    for a in range(2):
        xre = xs[a, 0]
        xim = xs[a, 1]
        for b in range(2):
            yre = ys[b, 0]
            yim = ys[b, 1]
            real_part = dot(xre, yre) + dot(xim, yim)
            imag_part = dot(xim, yre) - dot(xre, yim)
            for c, part in enumerate((real_part, imag_part)):
                padded = jnp.concatenate([part, jnp.zeros_like(part)], axis=1)
                sheared = pltpu.roll(padded, 0, 1, stride=1, stride_axis=0)
                row = (a * 2 + b) * 2 + c
                o_ref[slot, pl.ds(row, 1), :] = jnp.sum(sheared, axis=0, keepdims=True)


def block_rows(ref, chan, c, blk, width):
    return ref[chan, c, pl.ds(blk * width, width), :]


def lag_kernel(sel_ref, xraw_ref, xperm_ref, y00, y01, y10, y11, yperm_ref, o_ref, xs, ys):
    width = xperm_ref.shape[1]
    ys_in = ((y00, y01), (y10, y11))
    lags_into(
        lambda a, c: block_rows(xraw_ref, 0, c, a, width),
        lambda b, c: ys_in[b][c][0, 0, pl.ds(0, width), :],
        xperm_ref, yperm_ref, o_ref, 0, xs, ys,
    )


def start_relay(src_ref, dst_ref, send_sem, recv_sem):
    me = lax.axis_index("inp")
    fq = lax.axis_index("freq")
    onward = lax.bitwise_xor(me, 6)
    barrier = pltpu.get_barrier_semaphore()
    pl.semaphore_signal(barrier, inc=1, device_id=(onward, fq), device_id_type=MESH)
    pl.semaphore_wait(barrier, 1)
    copy = pltpu.make_async_remote_copy(
        src_ref=src_ref,
        dst_ref=dst_ref,
        send_sem=send_sem,
        recv_sem=recv_sem,
        device_id=(onward, fq),
        device_id_type=MESH,
    )
    copy.start()
    return copy


def relay_only_kernel(chunk_ref, prev_ref, relay_ref, send_sem, recv_sem):
    del prev_ref
    start_relay(chunk_ref, relay_ref, send_sem, recv_sem).wait()


def relay_own_kernel(chunk_ref, x_ref, xperm_ref, yperm_ref, o_ref, relay_ref, xs, ys, send_sem, recv_sem):
    width = xperm_ref.shape[1]
    copy = start_relay(chunk_ref, relay_ref, send_sem, recv_sem)
    for f in range(x_ref.shape[0]):
        lags_into(
            lambda a, c, f=f: block_rows(x_ref, f, c, a, width),
            lambda b, c, f=f: block_rows(x_ref, f, c, b, width),
            xperm_ref, yperm_ref, o_ref, f, xs, ys,
        )
    copy.wait()


def relay_kernel(x_ref, xperm_ref, y00, y01, y10, y11, yperm_ref, z_ref, zperm_ref, prev_ref,
                 o_ref, relay_ref, xs, ys, send_sem, recv_sem):
    del prev_ref
    width = xperm_ref.shape[1]
    me = lax.axis_index("inp")
    copy = start_relay(y11, relay_ref, send_sem, recv_sem)
    parity = lax.bitwise_and(lax.bitwise_xor(lax.shift_right_logical(me, 1), lax.shift_right_logical(me, 2)), 1)
    ys_in = ((y00, y01), (y10, y11))
    lags_into(
        lambda a, c: block_rows(x_ref, parity, c, a, width),
        lambda b, c: ys_in[b][c][0, 0, pl.ds(0, width), :],
        xperm_ref, yperm_ref, o_ref, 0, xs, ys,
    )
    lags_into(
        lambda a, c: block_rows(x_ref, lax.bitwise_and(me, 1), c, a, width),
        lambda b, c: block_rows(z_ref, 0, c, b, width),
        xperm_ref, zperm_ref, o_ref, 1, xs, ys,
    )
    copy.wait()


def relay_call(kernel, args, outs, n_lags, width, samples, collective_id, hbm_args=()):
    vmem = pl.BlockSpec(memory_space=pltpu.VMEM)
    hbm = pl.BlockSpec(memory_space=pl.ANY)
    out_specs = tuple(hbm for _ in outs)
    scratch = []
    if n_lags:
        outs = (jax.ShapeDtypeStruct((n_lags, 8, 2 * width), jnp.float32),) + outs
        out_specs = (vmem,) + out_specs
        scratch = [pltpu.VMEM((2, 2, width, samples), jnp.bfloat16)] * 2
    return pl.pallas_call(
        kernel,
        out_shape=outs,
        in_specs=[hbm if i in hbm_args else vmem for i in range(len(args))],
        out_specs=out_specs,
        scratch_shapes=scratch + [pltpu.SemaphoreType.DMA(()), pltpu.SemaphoreType.DMA(())],
        compiler_params=pltpu.CompilerParams(
            collective_id=collective_id, has_side_effects=True, vmem_limit_bytes=48 * 1024 * 1024
        ),
        cost_estimate=pl.CostEstimate(
            flops=max(n_lags, 1) * 4 * 24 * 2 * width * width * samples, transcendentals=0,
            bytes_accessed=4 * 2 * 4 * width * samples * 2,
        ),
    )(*args)


def pair_lags(sel, x_raw, x_perm, y_parts, y_perm, y_by_sel):
    n = sel.shape[0]
    _, _, rows_x, samples = x_raw.shape
    width = x_perm.shape[1]
    x_spec = pl.BlockSpec((1, 2, rows_x, samples), lambda i, s: (s[i], 0, 0, 0))
    if y_by_sel:
        y_specs = [
            pl.BlockSpec((1, 1, width, samples), lambda i, s, b=b, c=c: (s[i], c, b, 0))
            for b in range(2) for c in range(2)
        ]
        y_args = [y_parts] * 4
    else:
        y_specs = [
            pl.BlockSpec((1, 1) + part.shape[2:], lambda i, s: (0, 0, 0, 0)) for part in y_parts
        ]
        y_args = list(y_parts)
    perm_spec = pl.BlockSpec((2, width, width), lambda i, s: (0, 0, 0))
    out_spec = pl.BlockSpec((1, 8, 2 * width), lambda i, s: (i, 0, 0))
    flops = n * (16 + 8) * 2 * width * width * samples
    return pl.pallas_call(
        lag_kernel,
        out_shape=jax.ShapeDtypeStruct((n, 8, 2 * width), jnp.float32),
        grid_spec=pltpu.PrefetchScalarGridSpec(
            num_scalar_prefetch=1,
            grid=(n,),
            in_specs=[x_spec, perm_spec] + y_specs + [perm_spec],
            out_specs=out_spec,
            scratch_shapes=[
                pltpu.VMEM((2, 2, width, samples), x_raw.dtype),
                pltpu.VMEM((2, 2, width, samples), x_raw.dtype),
            ],
        ),
        compiler_params=pltpu.CompilerParams(vmem_limit_bytes=48 * 1024 * 1024),
        cost_estimate=pl.CostEstimate(
            flops=flops, transcendentals=0, bytes_accessed=n * 2 * 4 * width * samples * 2
        ),
    )(sel, x_raw, x_perm, *y_args, y_perm)


def scatter_kernel(dense_ref, out_ref, recv, send_sem, recv_sem):
    n = dense_ref.shape[0]
    me = lax.axis_index("inp")
    fq = lax.axis_index("freq")
    barrier = pltpu.get_barrier_semaphore()
    for o in range(1, n):
        pl.semaphore_signal(barrier, inc=1, device_id=(lax.rem(me + o, n), fq), device_id_type=MESH)
    pl.semaphore_wait(barrier, n - 1)
    copies = []
    for o in range(1, n):
        target = lax.rem(me + o, n)
        copy = pltpu.make_async_remote_copy(
            src_ref=dense_ref.at[target],
            dst_ref=recv.at[o - 1],
            send_sem=send_sem.at[o - 1],
            recv_sem=recv_sem.at[o - 1],
            device_id=(target, fq),
            device_id_type=MESH,
        )
        copy.start()
        copies.append(copy)
    for copy in copies:
        copy.wait()
    total = dense_ref[me]
    for o in range(n - 1):
        total = total + recv[o]
    out_ref[...] = total


def reduce_scatter(dense):
    n = dense.shape[0]
    slab = dense.shape[1:]
    return pl.pallas_call(
        scatter_kernel,
        out_shape=jax.ShapeDtypeStruct(slab, jnp.float32),
        in_specs=[pl.BlockSpec(memory_space=pltpu.VMEM)],
        out_specs=pl.BlockSpec(memory_space=pltpu.VMEM),
        scratch_shapes=[
            pltpu.VMEM((n - 1,) + slab, jnp.float32),
            pltpu.SemaphoreType.DMA((n - 1,)),
            pltpu.SemaphoreType.DMA((n - 1,)),
        ],
        compiler_params=pltpu.CompilerParams(collective_id=0, has_side_effects=True),
    )(dense)


def on_device(volts, position_input, tile_group):
    blocks, width = position_input.shape
    channels, _, rows, samples = volts.shape
    diffs = 2 * width - 1
    n_inp = lax.axis_size("inp")
    levels = n_inp.bit_length() - 1
    me = lax.axis_index("inp")

    pos_row = jnp.pad(position_input.reshape(-1), (0, samples - blocks * width))
    tg_flat = tile_group.reshape(-1)
    tg_row = jnp.pad(tg_flat, (0, samples - tg_flat.shape[0]))
    meta = jnp.stack([pos_row, tg_row]).astype(jnp.float32).astype(volts.dtype)
    meta = jnp.pad(meta[None], [(0, 1), (0, 14), (0, 0)])

    def chunks(chan):
        pick = lambda c, blk: jnp.where(chan == 1, volts[1, c, blk * width:(blk + 1) * width],
                                        volts[0, c, blk * width:(blk + 1) * width])
        parts = [pick(c, blk) for blk in range(2) for c in range(2)]
        parts[1] = jnp.concatenate([parts[1], meta[0]], axis=0)
        return [part[None, None] for part in parts]

    mine = [me & 1] + [((me >> 1) ^ (me >> 2)) & 1] * min(levels - 1, 2)
    mine += [(me >> bit) & 1 for bit in range(3, levels)]
    got1 = [lax.ppermute(part, "inp", [(i, i ^ 2) for i in range(n_inp)]) for part in chunks(1 - mine[1])]
    got0 = lax.ppermute(
        jnp.concatenate([jnp.where(mine[0] == 0, volts[1], volts[0]), meta], axis=1)[None],
        "inp",
        [(i, i ^ 1) for i in range(n_inp)],
    )
    ids = jnp.arange(width, dtype=jnp.int32)

    def one_hot(pos, reverse):
        if reverse:
            pos = pos[:, ::-1]
        return (pos[:, :, None] == ids[None, None, :]).astype(volts.dtype)

    perm = one_hot(position_input, False)
    perm_rev = one_hot(position_input, True)

    groups_all = RG_DEV * n_inp
    group_ids = jnp.arange(groups_all, dtype=jnp.int32)
    chan_ids = jnp.arange(channels, dtype=jnp.int32)

    chunk_shape = lambda k: (jax.ShapeDtypeStruct(got1[k].shape, got1[k].dtype),)
    lag0, relay0 = relay_call(
        relay_own_kernel, (got1[0], volts, perm, perm_rev), chunk_shape(0), channels, width, samples, 1, (0,)
    )
    (relay1,) = relay_call(relay_only_kernel, (got1[1], relay0), chunk_shape(1), 0, width, samples, 2, (0, 1))
    (relay2,) = relay_call(relay_only_kernel, (got1[2], relay1), chunk_shape(2), 0, width, samples, 3, (0, 1))
    relayed = [relay0, relay1, relay2]
    lag0 = lag0.reshape(channels, 2, 2, 2, 2 * width)
    center = (jnp.arange(2 * width) == width - 1)
    same = jnp.eye(2, dtype=bool)
    lag0 = jnp.where(same[None, :, :, None, None] & center[None, None, None, None, :], 0.0, lag0)
    def flip_lags(lag):
        return jnp.concatenate([jnp.flip(lag[..., :diffs], axis=-1), jnp.zeros_like(lag[..., diffs:])], axis=-1)

    contrib_w = []
    contrib_v = []
    w0 = (tile_group[:, 0, :, None] == group_ids).astype(jnp.float32)
    f0 = (chan_ids[:, None] == chan_ids[None, :]).astype(jnp.float32)
    contrib_w.append(jnp.einsum("abg,fh->fabgh", w0, f0).reshape(-1, groups_all, channels))
    contrib_v.append(flip_lags(lag0).reshape(-1, 2, 2 * width))
    sign = jnp.array([1.0, -1.0], jnp.float32)

    def meta_of(slab, row):
        got_pos = slab[0, 0, row, : blocks * width].astype(jnp.int32).reshape(blocks, width)
        got_tg = slab[0, 0, row + 1, : tg_flat.shape[0]].astype(jnp.int32).reshape(tile_group.shape)
        return one_hot(got_pos, True), got_tg

    perm1, tg1 = meta_of(got1[1], width)
    perm0, tg0 = meta_of(got0, rows)
    lag10, relay_last = relay_call(
        relay_kernel, (volts, perm, *got1, perm1, got0, perm0, relay2), chunk_shape(3), 2, width, samples, 4, (9,)
    )
    perm2, tg2 = meta_of(relayed[1], width)
    lag2 = pair_lags(mine[2][None].astype(jnp.int32), volts, perm, relayed + [relay_last], perm2, False)
    level_lags = {0: (lag10[1], tg0), 1: (lag10[0], tg1), 2: (lag2[0], tg2)}
    for bit in range(levels):
        lag, got_tg = level_lags[bit]
        lag = lag.reshape(2, 2, 2, 2 * width)
        fmask = (chan_ids == mine[bit]).astype(jnp.float32)
        w_direct = (tile_group[:, bit + 1, :, None] == group_ids).astype(jnp.float32)
        w_trans = jnp.swapaxes((got_tg[:, bit + 1, :, None] == group_ids).astype(jnp.float32), 0, 1)
        contrib_w.append(jnp.einsum("abg,f->abgf", w_direct, fmask).reshape(-1, groups_all, channels))
        contrib_v.append(flip_lags(lag).reshape(-1, 2, 2 * width))
        contrib_w.append(jnp.einsum("abg,f->abgf", w_trans, fmask).reshape(-1, groups_all, channels))
        contrib_v.append((lag * sign[:, None]).reshape(-1, 2, 2 * width))
    dense = jnp.einsum(
        "ngf,nck->gfck", jnp.concatenate(contrib_w), jnp.concatenate(contrib_v), precision=HIGH
    )
    dense = dense * (1.0 / samples)
    dense = dense.reshape((n_inp, RG_DEV) + dense.shape[1:])
    return reduce_scatter(dense)[..., :diffs]


def solution(mesh):
    return jax.shard_map(
        on_device,
        mesh=mesh,
        in_specs=(P("freq", None, "inp", None), P("inp", None), P("inp", None, None)),
        out_specs=P("inp", "freq", None, None),
        check_vma=False,
    )
```

```python
import jax
import jax.numpy as jnp
from jax import lax
from jax.experimental import pallas as pl
from jax.experimental.pallas import tpu as pltpu
from jax.sharding import PartitionSpec as P

RG_DEV = 8
HIGH = lax.Precision.HIGHEST
NT = (((1,), (1,)), ((), ()))
MESH = pl.DeviceIdType.MESH


def lags_into(get_x, get_y, xperm_ref, yperm_ref, o_ref, slot, xs, ys):
    for blk in range(2):
        for c in range(2):
            xs[blk, c] = jnp.dot(xperm_ref[blk], get_x(blk, c), preferred_element_type=jnp.float32).astype(xs.dtype)
            ys[blk, c] = jnp.dot(yperm_ref[blk], get_y(blk, c), preferred_element_type=jnp.float32).astype(ys.dtype)
    dot = lambda u, v: lax.dot_general(u, v, NT, preferred_element_type=jnp.float32)
    for a in range(2):
        xre = xs[a, 0]
        xim = xs[a, 1]
        for b in range(2):
            yre = ys[b, 0]
            yim = ys[b, 1]
            real_part = dot(xre, yre) + dot(xim, yim)
            imag_part = dot(xim, yre) - dot(xre, yim)
            for c, part in enumerate((real_part, imag_part)):
                padded = jnp.concatenate([part, jnp.zeros_like(part)], axis=1)
                sheared = pltpu.roll(padded, 0, 1, stride=1, stride_axis=0)
                row = (a * 2 + b) * 2 + c
                o_ref[slot, pl.ds(row, 1), :] = jnp.sum(sheared, axis=0, keepdims=True)


def block_rows(ref, chan, c, blk, width):
    return ref[chan, c, pl.ds(blk * width, width), :]


def lag_kernel(sel_ref, xraw_ref, xperm_ref, y00, y01, y10, y11, yperm_ref, o_ref, xs, ys):
    width = xperm_ref.shape[1]
    ys_in = ((y00, y01), (y10, y11))
    lags_into(
        lambda a, c: block_rows(xraw_ref, 0, c, a, width),
        lambda b, c: ys_in[b][c][0, 0, pl.ds(0, width), :],
        xperm_ref, yperm_ref, o_ref, 0, xs, ys,
    )


def start_relay(src_ref, dst_ref, send_sem, recv_sem):
    me = lax.axis_index("inp")
    fq = lax.axis_index("freq")
    onward = lax.bitwise_xor(me, 6)
    barrier = pltpu.get_barrier_semaphore()
    pl.semaphore_signal(barrier, inc=1, device_id=(onward, fq), device_id_type=MESH)
    pl.semaphore_wait(barrier, 1)
    copy = pltpu.make_async_remote_copy(
        src_ref=src_ref,
        dst_ref=dst_ref,
        send_sem=send_sem,
        recv_sem=recv_sem,
        device_id=(onward, fq),
        device_id_type=MESH,
    )
    copy.start()
    return copy


def relay_only_kernel(chunk_ref, prev_ref, relay_ref, send_sem, recv_sem):
    del prev_ref
    start_relay(chunk_ref, relay_ref, send_sem, recv_sem).wait()


def relay_own_kernel(chunk_ref, x_ref, xperm_ref, yperm_ref, o_ref, relay_ref, xs, ys, send_sem, recv_sem):
    width = xperm_ref.shape[1]
    copy = start_relay(chunk_ref, relay_ref, send_sem, recv_sem)
    for f in range(x_ref.shape[0]):
        lags_into(
            lambda a, c, f=f: block_rows(x_ref, f, c, a, width),
            lambda b, c, f=f: block_rows(x_ref, f, c, b, width),
            xperm_ref, yperm_ref, o_ref, f, xs, ys,
        )
    copy.wait()


def relay_kernel(x_ref, xperm_ref, y00, y01, y10, y11, yperm_ref, z_ref, zperm_ref, r00, r01, r10, rperm_ref,
                 o_ref, relay_ref, xs, ys, send_sem, recv_sem):
    width = xperm_ref.shape[1]
    me = lax.axis_index("inp")
    copy = start_relay(y11, relay_ref, send_sem, recv_sem)
    parity = lax.bitwise_and(lax.bitwise_xor(lax.shift_right_logical(me, 1), lax.shift_right_logical(me, 2)), 1)
    ys_in = ((y00, y01), (y10, y11))
    lags_into(
        lambda a, c: block_rows(x_ref, parity, c, a, width),
        lambda b, c: ys_in[b][c][0, 0, pl.ds(0, width), :],
        xperm_ref, yperm_ref, o_ref, 0, xs, ys,
    )
    lags_into(
        lambda a, c: block_rows(x_ref, lax.bitwise_and(me, 1), c, a, width),
        lambda b, c: block_rows(z_ref, 0, c, b, width),
        xperm_ref, zperm_ref, o_ref, 1, xs, ys,
    )
    copy.wait()
    relayed = ((r00, r01), (r10, relay_ref))
    lags_into(
        lambda a, c: block_rows(x_ref, parity, c, a, width),
        lambda b, c: relayed[b][c][0, 0, pl.ds(0, width), :],
        xperm_ref, rperm_ref, o_ref, 2, xs, ys,
    )


def relay_call(kernel, args, outs, n_lags, width, samples, collective_id):
    vmem = pl.BlockSpec(memory_space=pltpu.VMEM)
    scratch = []
    if n_lags:
        outs = (jax.ShapeDtypeStruct((n_lags, 8, 2 * width), jnp.float32),) + outs
        scratch = [pltpu.VMEM((2, 2, width, samples), jnp.bfloat16)] * 2
    return pl.pallas_call(
        kernel,
        out_shape=outs,
        in_specs=[vmem] * len(args),
        out_specs=tuple(vmem for _ in outs),
        scratch_shapes=scratch + [pltpu.SemaphoreType.DMA(()), pltpu.SemaphoreType.DMA(())],
        compiler_params=pltpu.CompilerParams(
            collective_id=collective_id, has_side_effects=True, vmem_limit_bytes=48 * 1024 * 1024
        ),
        cost_estimate=pl.CostEstimate(
            flops=max(n_lags, 1) * 4 * 24 * 2 * width * width * samples, transcendentals=0,
            bytes_accessed=4 * 2 * 4 * width * samples * 2,
        ),
    )(*args)


def pair_lags(sel, x_raw, x_perm, y_parts, y_perm, y_by_sel):
    n = sel.shape[0]
    _, _, rows_x, samples = x_raw.shape
    width = x_perm.shape[1]
    x_spec = pl.BlockSpec((1, 2, rows_x, samples), lambda i, s: (s[i], 0, 0, 0))
    if y_by_sel:
        y_specs = [
            pl.BlockSpec((1, 1, width, samples), lambda i, s, b=b, c=c: (s[i], c, b, 0))
            for b in range(2) for c in range(2)
        ]
        y_args = [y_parts] * 4
    else:
        y_specs = [
            pl.BlockSpec((1, 1) + part.shape[2:], lambda i, s: (0, 0, 0, 0)) for part in y_parts
        ]
        y_args = list(y_parts)
    perm_spec = pl.BlockSpec((2, width, width), lambda i, s: (0, 0, 0))
    out_spec = pl.BlockSpec((1, 8, 2 * width), lambda i, s: (i, 0, 0))
    flops = n * (16 + 8) * 2 * width * width * samples
    return pl.pallas_call(
        lag_kernel,
        out_shape=jax.ShapeDtypeStruct((n, 8, 2 * width), jnp.float32),
        grid_spec=pltpu.PrefetchScalarGridSpec(
            num_scalar_prefetch=1,
            grid=(n,),
            in_specs=[x_spec, perm_spec] + y_specs + [perm_spec],
            out_specs=out_spec,
            scratch_shapes=[
                pltpu.VMEM((2, 2, width, samples), x_raw.dtype),
                pltpu.VMEM((2, 2, width, samples), x_raw.dtype),
            ],
        ),
        compiler_params=pltpu.CompilerParams(vmem_limit_bytes=48 * 1024 * 1024),
        cost_estimate=pl.CostEstimate(
            flops=flops, transcendentals=0, bytes_accessed=n * 2 * 4 * width * samples * 2
        ),
    )(sel, x_raw, x_perm, *y_args, y_perm)


def scatter_kernel(dense_ref, out_ref, recv, send_sem, recv_sem):
    n = dense_ref.shape[0]
    me = lax.axis_index("inp")
    fq = lax.axis_index("freq")
    barrier = pltpu.get_barrier_semaphore()
    for o in range(1, n):
        pl.semaphore_signal(barrier, inc=1, device_id=(lax.rem(me + o, n), fq), device_id_type=MESH)
    pl.semaphore_wait(barrier, n - 1)
    copies = []
    for o in range(1, n):
        target = lax.rem(me + o, n)
        copy = pltpu.make_async_remote_copy(
            src_ref=dense_ref.at[target],
            dst_ref=recv.at[o - 1],
            send_sem=send_sem.at[o - 1],
            recv_sem=recv_sem.at[o - 1],
            device_id=(target, fq),
            device_id_type=MESH,
        )
        copy.start()
        copies.append(copy)
    for copy in copies:
        copy.wait()
    total = dense_ref[me]
    for o in range(n - 1):
        total = total + recv[o]
    out_ref[...] = total


def reduce_scatter(dense):
    n = dense.shape[0]
    slab = dense.shape[1:]
    return pl.pallas_call(
        scatter_kernel,
        out_shape=jax.ShapeDtypeStruct(slab, jnp.float32),
        in_specs=[pl.BlockSpec(memory_space=pltpu.VMEM)],
        out_specs=pl.BlockSpec(memory_space=pltpu.VMEM),
        scratch_shapes=[
            pltpu.VMEM((n - 1,) + slab, jnp.float32),
            pltpu.SemaphoreType.DMA((n - 1,)),
            pltpu.SemaphoreType.DMA((n - 1,)),
        ],
        compiler_params=pltpu.CompilerParams(collective_id=0, has_side_effects=True),
    )(dense)


def on_device(volts, position_input, tile_group):
    blocks, width = position_input.shape
    channels, _, rows, samples = volts.shape
    diffs = 2 * width - 1
    n_inp = lax.axis_size("inp")
    levels = n_inp.bit_length() - 1
    me = lax.axis_index("inp")

    pos_row = jnp.pad(position_input.reshape(-1), (0, samples - blocks * width))
    tg_flat = tile_group.reshape(-1)
    tg_row = jnp.pad(tg_flat, (0, samples - tg_flat.shape[0]))
    meta = jnp.stack([pos_row, tg_row]).astype(jnp.float32).astype(volts.dtype)
    meta = jnp.pad(meta[None], [(0, 1), (0, 14), (0, 0)])

    def chunks(chan):
        pick = lambda c, blk: jnp.where(chan == 1, volts[1, c, blk * width:(blk + 1) * width],
                                        volts[0, c, blk * width:(blk + 1) * width])
        parts = [pick(c, blk) for blk in range(2) for c in range(2)]
        parts[0] = jnp.concatenate([parts[0], meta[0]], axis=0)
        return [part[None, None] for part in parts]

    mine = [me & 1] + [((me >> 1) ^ (me >> 2)) & 1] * min(levels - 1, 2)
    mine += [(me >> bit) & 1 for bit in range(3, levels)]
    got1 = [lax.ppermute(part, "inp", [(i, i ^ 2) for i in range(n_inp)]) for part in chunks(1 - mine[1])]
    got0 = lax.ppermute(
        jnp.concatenate([jnp.where(mine[0] == 0, volts[1], volts[0]), meta], axis=1)[None],
        "inp",
        [(i, i ^ 1) for i in range(n_inp)],
    )
    ids = jnp.arange(width, dtype=jnp.int32)

    def one_hot(pos, reverse):
        if reverse:
            pos = pos[:, ::-1]
        return (pos[:, :, None] == ids[None, None, :]).astype(volts.dtype)

    perm = one_hot(position_input, False)
    perm_rev = one_hot(position_input, True)

    groups_all = RG_DEV * n_inp
    group_ids = jnp.arange(groups_all, dtype=jnp.int32)
    chan_ids = jnp.arange(channels, dtype=jnp.int32)

    chunk_shape = lambda k: (jax.ShapeDtypeStruct(got1[k].shape, got1[k].dtype),)
    lag0, relay0 = relay_call(
        relay_own_kernel, (got1[0], volts, perm, perm_rev), chunk_shape(0), channels, width, samples, 1
    )
    (relay1,) = relay_call(relay_only_kernel, (got1[1], relay0), chunk_shape(1), 0, width, samples, 2)
    (relay2,) = relay_call(relay_only_kernel, (got1[2], relay1), chunk_shape(2), 0, width, samples, 3)
    relayed = [relay0, relay1, relay2]
    lag0 = lag0.reshape(channels, 2, 2, 2, 2 * width)
    center = (jnp.arange(2 * width) == width - 1)
    same = jnp.eye(2, dtype=bool)
    lag0 = jnp.where(same[None, :, :, None, None] & center[None, None, None, None, :], 0.0, lag0)
    contrib_w = []
    contrib_v = []
    w0 = (tile_group[:, 0, :, None] == group_ids).astype(jnp.float32)
    f0 = (chan_ids[:, None] == chan_ids[None, :]).astype(jnp.float32)
    contrib_w.append(jnp.einsum("abg,fh->fabgh", w0, f0).reshape(-1, groups_all, channels))
    contrib_v.append(jnp.flip(lag0[..., :diffs], axis=-1).reshape(-1, 2, diffs))
    sign = jnp.array([1.0, -1.0], jnp.float32)

    def meta_of(slab, row):
        got_pos = slab[0, 0, row, : blocks * width].astype(jnp.int32).reshape(blocks, width)
        got_tg = slab[0, 0, row + 1, : tg_flat.shape[0]].astype(jnp.int32).reshape(tile_group.shape)
        return one_hot(got_pos, True), got_tg

    perm1, tg1 = meta_of(got1[0], width)
    perm0, tg0 = meta_of(got0, rows)
    perm2, tg2 = meta_of(relayed[0], width)
    lag10, _ = relay_call(
        relay_kernel, (volts, perm, *got1, perm1, got0, perm0, *relayed, perm2), chunk_shape(3), 3, width, samples, 4
    )
    level_lags = {0: (lag10[1], tg0), 1: (lag10[0], tg1), 2: (lag10[2], tg2)}
    for bit in range(levels):
        lag, got_tg = level_lags[bit]
        lag = lag.reshape(2, 2, 2, 2 * width)[..., :diffs]
        fmask = (chan_ids == mine[bit]).astype(jnp.float32)
        w_direct = (tile_group[:, bit + 1, :, None] == group_ids).astype(jnp.float32)
        w_trans = jnp.swapaxes((got_tg[:, bit + 1, :, None] == group_ids).astype(jnp.float32), 0, 1)
        contrib_w.append(jnp.einsum("abg,f->abgf", w_direct, fmask).reshape(-1, groups_all, channels))
        contrib_v.append(jnp.flip(lag, axis=-1).reshape(-1, 2, diffs))
        contrib_w.append(jnp.einsum("abg,f->abgf", w_trans, fmask).reshape(-1, groups_all, channels))
        contrib_v.append((lag * sign[:, None]).reshape(-1, 2, diffs))
    dense = jnp.einsum(
        "ngf,nck->gfck", jnp.concatenate(contrib_w), jnp.concatenate(contrib_v), precision=HIGH
    )
    dense = dense * (1.0 / samples)
    dense = jnp.pad(dense, [(0, 0)] * 3 + [(0, 1)])
    dense = dense.reshape((n_inp, RG_DEV) + dense.shape[1:])
    return reduce_scatter(dense)[..., :diffs]


def solution(mesh):
    return jax.shard_map(
        on_device,
        mesh=mesh,
        in_specs=(P("freq", None, "inp", None), P("inp", None), P("inp", None, None)),
        out_specs=P("inp", "freq", None, None),
        check_vma=False,
    )
```
